256 devices in a mesh: ctx: 32 (over z, x), head: 4 (over y), dp: 2 (over core).
Axes of the slice: x: 4, y: 4, z: 8, core: 2. Of those that a mesh axis runs over, the one named last changes fastest.
Arguments:
- query_raw: bfloat16 [32768, 2048], P(('dp', 'ctx', 'head')), parts along dimension 0, may hold values from -6 to 6
- key_raw: bfloat16 [32768, 2048], P(('dp', 'ctx', 'head')), parts along dimension 0, may hold values from -6 to 6
- value_raw: bfloat16 [32768, 2048], P(('dp', 'ctx', 'head')), parts along dimension 0, may hold values from -6 to 6
- log_decay: bfloat16 [32768, 2048], P(('dp', 'ctx', 'head')), parts along dimension 0, may hold values from -1 to 0, as said below
- beta: bfloat16 [32768, 16], P(('dp', 'ctx', 'head')), parts along dimension 0, may hold values from 0.0029 to 1
- conv_weight: float32 [3, 4, 2048], replicated, may hold values from -3 to 3
- out_gate: bfloat16 [32768, 2048], P(('dp', 'ctx', 'head')), parts along dimension 0, may hold values from -6 to 6
- norm_gain: float32 [128], replicated, may hold values from 0.1 to 1.9
Outputs:
- mixed: bfloat16 [32768, 2048], P(('dp', 'ctx', 'head')), parts along dimension 0
The draws below stay inside these ranges and needn't reach their ends.
There are 2 independent parts, one for each index of `dp`. The reference program is written for one: setup_inputs(seed, part) draws one part's arguments, and reference() takes and returns one part's arrays. A program takes and returns all parts, laid end to end along the dimension named above; an argument that names none is the same for every part. Nothing has to cross between parts.
Inputs may be any that keep to these rules, and one draw needn't show every extreme that they name: `log_decay`: logarithms (all <= 0) of the decay factors of the state.
All inputs are finite; a program needn't handle non-finite values.
Results may differ from the reference program's by a relative error of at most 0.013.
Values may be sent and summed in bfloat16 or wider, within the bound.
A program may use at most 64 MiB of HBM per device.

```python
import jax
import jax.numpy as jnp
from jax import lax

HEAD_COUNT = 16
HEAD_WIDTH = 128
CONV = 4
STRETCH = 64
HD = 2048
SPAN = 512
TOKEN_COUNT = 16384


def head_order(key):
    return jax.random.permutation(jax.random.fold_in(key, 101), HEAD_COUNT)


def draw_key_raw(key, part):
    input_flows = jax.random.split(jax.random.fold_in(key, 404), 3)
    magnitude = jax.random.uniform(input_flows[0], (1, HEAD_COUNT * HEAD_WIDTH), jnp.float32, 1.0, 2.5)
    sign_pick = jax.random.randint(input_flows[1], (1, HEAD_COUNT * HEAD_WIDTH), 0, 2).astype(jnp.float32) * 2.0 - 1.0
    jitter = jax.random.normal(input_flows[2], (TOKEN_COUNT, HEAD_COUNT * HEAD_WIDTH), jnp.float32)
    final_output = jnp.clip(magnitude * sign_pick + jitter, -6.0, 6.0)
    return final_output.astype(jnp.bfloat16)


def draw_beta(key, part):
    order = head_order(key)
    stride = 2
    strong_heads = order % stride == 0
    input_flows = jax.random.split(jax.random.fold_in(key, 202), 2)
    strong_draw = jnp.exp(jax.random.uniform(input_flows[0], (TOKEN_COUNT, HEAD_COUNT), jnp.float32, jnp.log(0.05), jnp.log(1.0)))
    weak_draw = jnp.exp(jax.random.uniform(input_flows[1], (TOKEN_COUNT, HEAD_COUNT), jnp.float32, jnp.log(0.003), jnp.log(0.03)))
    final_output = jnp.where(strong_heads[None, :], strong_draw, weak_draw)
    return final_output.astype(jnp.bfloat16)


def draw_log_decay(key, part):
    input_flows = jax.random.split(jax.random.fold_in(key, 303), 8)
    order = head_order(key)
    fast_count = HEAD_COUNT // 2
    rough_low = 0.5
    rough_high = 1.5
    fast_heads = order < fast_count
    fast_rate = 1.0 / jax.random.uniform(input_flows[1], (HEAD_COUNT, 1), jnp.float32, 30.0, 50.0)
    slow_rate = jnp.exp(jax.random.uniform(input_flows[2], (HEAD_COUNT, 1), jnp.float32, jnp.log(0.05), jnp.log(0.3))) / TOKEN_COUNT
    channel_factor = jnp.exp(jax.random.uniform(input_flows[3], (HEAD_COUNT, HEAD_WIDTH), jnp.float32, jnp.log(0.5), jnp.log(2.0)))
    baseline_rate = (jnp.where(fast_heads[:, None], fast_rate, slow_rate) * channel_factor).reshape(1, HEAD_COUNT * HEAD_WIDTH)
    block_count = TOKEN_COUNT // SPAN
    block_multiplier = jnp.exp(jax.random.uniform(input_flows[4], (block_count, HEAD_COUNT * HEAD_WIDTH), jnp.float32, jnp.log(0.5), jnp.log(2.0)))
    block_multiplier = jnp.repeat(block_multiplier, SPAN, axis=0)
    jaggedness = jax.random.uniform(input_flows[5], (TOKEN_COUNT, HEAD_COUNT * HEAD_WIDTH), jnp.float32, rough_low, rough_high)
    spike_position = jax.random.randint(input_flows[6], (2, HEAD_COUNT), 0, TOKEN_COUNT)
    spike_penalty = jax.random.uniform(input_flows[7], (2, HEAD_COUNT), jnp.float32, 0.223, 0.693)
    positions = jnp.arange(TOKEN_COUNT)[:, None]
    spike_events = jnp.where(positions == spike_position[0][None, :], spike_penalty[0][None, :], 0.0)
    spike_events = spike_events + jnp.where(positions == spike_position[1][None, :], spike_penalty[1][None, :], 0.0)
    spike_events = jnp.repeat(spike_events, HEAD_WIDTH, axis=1)
    final_output = -(baseline_rate * block_multiplier * jaggedness) - spike_events
    return final_output.astype(jnp.bfloat16)


def levels(stream_key, dims, pieces, smallest, high):
    level, own = 1.0, jax.random.fold_in(stream_key, 6)
    for axis_at, parts in pieces:
        draws = jnp.exp(jax.random.uniform(jax.random.fold_in(own, axis_at), (parts,), jnp.float32, smallest / len(pieces), high / len(pieces)))
        level = level * jnp.repeat(draws, dims[axis_at] // parts).reshape([-1 if axis == axis_at else 1 for axis in range(len(dims))])
    return level


def noise(own_key, shape, scale, limit, cuts=(), held_as=jnp.bfloat16):
    drawn = jax.random.normal(own_key, shape, jnp.float32) * scale
    if len(cuts) > 0:
        drawn = levels(own_key, shape, cuts, -0.22, 0.18) * drawn
    return jnp.clip(drawn, min=-limit, max=limit).astype(held_as)


def setup_inputs(seed: int = 0, part: int = 0) -> dict:
    splits = jax.random.split(jax.random.key(seed), 9)
    own_keys = jax.random.split(jax.random.fold_in(splits[8], part), 9)
    query_raw = noise(own_keys[0], (TOKEN_COUNT, HD), 1.0, 6.0, ((0, 128),))
    key_raw = draw_key_raw(jax.random.fold_in(jax.random.fold_in(splits[8], part), 71), part)
    value_raw = noise(own_keys[2], (TOKEN_COUNT, HD), 1.0, 6.0, ((0, 128),))
    log_decay = draw_log_decay(jax.random.fold_in(jax.random.fold_in(splits[8], part), 71), part)
    beta = draw_beta(jax.random.fold_in(jax.random.fold_in(splits[8], part), 71), part)
    conv_weight = noise(splits[5], (3, CONV, HD), CONV ** -0.5, 3.0, (), jnp.float32)
    out_gate = noise(own_keys[6], (TOKEN_COUNT, HD), 1.5, 6.0, ((0, 128),))
    norm_gain = jnp.clip(1.0 + 0.18 * jax.random.normal(splits[7], (HEAD_WIDTH,), jnp.float32), 0.1, 1.9)
    return dict(query_raw=query_raw, key_raw=key_raw, value_raw=value_raw, log_decay=log_decay, beta=beta, conv_weight=conv_weight, out_gate=out_gate, norm_gain=norm_gain)


def matmul(left, right):
    return jnp.einsum('...ij,...jk->...ik', left, right, precision=lax.Precision.HIGHEST)

def short_conv(values_in, rim_rows, taps):
    count = values_in.shape[0]
    width = taps.shape[0]
    padded = jnp.concatenate([rim_rows, values_in], 0).astype(jnp.float32)
    total = taps[0] * padded[0:count]
    for offset in range(1, width):
        total = total + taps[offset] * padded[offset:offset + count]
    return jax.nn.silu(total).astype(jnp.bfloat16)

def block_terms(query, keys, values, log_gate, rates):
    keys = keys * lax.rsqrt(lax.optimization_barrier(jnp.sum(keys * keys, -1, keepdims=True)) + 1e-06)
    cumul = jnp.cumsum(log_gate, axis=-2)
    last_cum = cumul[..., -1:, :]
    query_up = query * jnp.exp(cumul)
    key_up = keys * jnp.exp(cumul)
    key_down = keys * jnp.exp(-cumul)
    key_end = keys * jnp.exp(last_cum - cumul)
    length = query.shape[-2]
    positions = jnp.arange(length)
    strict = positions[:, None] > positions[None, :]
    weak = positions[:, None] >= positions[None, :]
    inner = jnp.einsum('...cd,...jd->...cj', key_up, key_down, precision=lax.Precision.HIGHEST)
    unit_lower = jnp.eye(length, dtype=jnp.float32) + jnp.where(strict, inner * rates[..., :, None], 0.0)
    right_side = jnp.concatenate([rates[..., None] * values, rates[..., None] * key_up], -1)
    solved = lax.linalg.triangular_solve(unit_lower, right_side, left_side=True, lower=True, unit_diagonal=True)
    width = values.shape[-1]
    update_rows = solved[..., :width]
    correct_rows = solved[..., width:]
    scores = jnp.where(weak, jnp.einsum('...cd,...jd->...cj', query_up, key_down, precision=lax.Precision.HIGHEST), 0.0)
    return (query_up, key_end, update_rows, correct_rows, scores, last_cum)

def finish(attention, gate_logits, gain):
    rows_count = attention.shape[0]
    heads_view = attention.astype(jnp.float32).reshape(rows_count, -1, HEAD_WIDTH)
    scale = lax.rsqrt(lax.optimization_barrier(jnp.mean(heads_view * heads_view, -1, keepdims=True)) + 1e-05)
    gate_view = jax.nn.sigmoid(gate_logits.astype(jnp.float32).reshape(rows_count, -1, HEAD_WIDTH))
    final_output = heads_view * scale * gain * gate_view
    return final_output.reshape(rows_count, -1).astype(jnp.bfloat16)

def reference(query_raw, key_raw, value_raw, log_decay, beta, conv_weight, out_gate, norm_gain):
    zero_rim = jnp.zeros((CONV - 1, HEAD_COUNT * HEAD_WIDTH), jnp.bfloat16)
    query_in = short_conv(query_raw, zero_rim, conv_weight[0])
    key_in = short_conv(key_raw, zero_rim, conv_weight[1])
    value_in = short_conv(value_raw, zero_rim, conv_weight[2])
    blocks_count = TOKEN_COUNT // STRETCH

    def blocks(array):
        return array.reshape(blocks_count, STRETCH, array.shape[1])

    def heads_first(array):
        return array.astype(jnp.float32).reshape(STRETCH, HEAD_COUNT, HEAD_WIDTH).transpose(1, 0, 2)

    def advance(state, inputs):
        query_c, key_c, value_c, gate_c, rate_c = inputs
        rates = rate_c.astype(jnp.float32).transpose(1, 0)
        query_up, key_end, update_rows, correct_rows, scores, last_cum = block_terms(heads_first(query_c), heads_first(key_c), heads_first(value_c), heads_first(gate_c), rates)
        written = update_rows - matmul(correct_rows, state)
        output = matmul(query_up, state) + matmul(scores, written)
        new_state = jnp.exp(last_cum)[:, 0, :, None] * state + jnp.einsum('hcd,hce->hde', key_end, written, precision=lax.Precision.HIGHEST)
        return (new_state, output.transpose(1, 0, 2).reshape(STRETCH, HEAD_COUNT * HEAD_WIDTH).astype(jnp.bfloat16))
    start_state = jnp.zeros((HEAD_COUNT, HEAD_WIDTH, HEAD_WIDTH), jnp.float32)
    _, attention = lax.scan(advance, start_state, (blocks(query_in), blocks(key_in), blocks(value_in), blocks(log_decay), blocks(beta)))
    attention = attention.reshape(TOKEN_COUNT, HEAD_COUNT * HEAD_WIDTH)
    return finish(attention, out_gate, norm_gain)
```

```python
import functools

import jax
import jax.numpy as jnp
from jax import lax
from jax.experimental import pallas as pl
from jax.experimental.pallas import tpu as pltpu
from jax.sharding import PartitionSpec as P

MESH = pl.DeviceIdType.MESH
WIDTH = 128
HEADS = 16
SIDE = 4
F32 = jnp.float32
BF16 = jnp.bfloat16


def dot(a, b):
    return jnp.dot(a, b, preferred_element_type=F32)


def dot_nt(a, b):
    return lax.dot_general(a, b, (((1,), (1,)), ((), ())), preferred_element_type=F32)


def dot_tn(a, b):
    return lax.dot_general(a, b, (((0,), (0,)), ((), ())), preferred_element_type=F32)


def lanes_of(index):
    return pl.ds(pl.multiple_of(index * WIDTH, WIDTH), WIDTH)


def silu(u):
    return u / (1.0 + jnp.exp(-u))


def compose(first, second):
    return first.astype(F32) - dot(second[:, :WIDTH], first) + second.astype(F32)


def apply(step, state):
    return state.astype(F32) - dot(step[:, :WIDTH], state) + step[:, WIDTH:].astype(F32)


def kernel(
    depth,
    query_hbm,
    key_hbm,
    value_hbm,
    decay_hbm,
    gate_hbm,
    beta_ref,
    taps_ref,
    gain_ref,
    out_ref,
    query_in,
    key_in,
    value_in,
    decay_in,
    gate_in,
    rim,
    query_mid,
    key_mid,
    key_down,
    key_end,
    value_rate,
    edge,
    vectors,
    inner_out,
    query_state,
    level,
    send,
    recv,
    tree,
    state_in,
    state_out,
    starts,
    got,
    load_sem,
    rim_send,
    rim_recv,
    up_send,
    up_recv,
    chain_send,
    chain_recv,
    down_send,
    down_recv,
):
    ctx, y = lax.axis_index("ctx"), lax.axis_index("head")
    x, z = lax.rem(ctx, SIDE), lax.div(ctx, SIDE)
    place = x * SIDE + y
    mine = y * SIDE + x
    total = depth * SIDE * SIDE
    linear = ctx * SIDE + y
    after = lax.rem(linear + 1, total)
    before = lax.rem(linear + total - 1, total)

    def device(cx, cy):
        return {"ctx": cx, "head": cy}

    def in_plane(px, py):
        return device(z * SIDE + px, py)

    z_after = device(lax.rem(z + 1, depth) * SIDE + x, y)
    z_before = device(lax.rem(z + depth - 1, depth) * SIDE + x, y)
    token_after = device(lax.div(after, SIDE), lax.rem(after, SIDE))
    token_before = device(lax.div(before, SIDE), lax.rem(before, SIDE))

    barrier = pltpu.get_barrier_semaphore()
    for dx in range(SIDE):
        for dy in range(SIDE):
            if dx or dy:
                pl.semaphore_signal(
                    barrier,
                    inc=1,
                    device_id=in_plane(lax.rem(x + dx, SIDE), lax.rem(y + dy, SIDE)),
                    device_id_type=MESH,
                )
    for other in (z_after, z_before, token_after, token_before):
        pl.semaphore_signal(barrier, inc=1, device_id=other, device_id_type=MESH)

    loads = [
        pltpu.make_async_copy(source, target, load_sem.at[i])
        for i, (source, target) in enumerate(
            (
                (decay_hbm, decay_in),
                (query_hbm, query_in),
                (key_hbm, key_in),
                (value_hbm, value_in),
                (gate_hbm, gate_in),
            )
        )
    ]
    for load in loads:
        load.start()

    row = lax.broadcasted_iota(jnp.int32, (WIDTH, WIDTH), 0)
    col = lax.broadcasted_iota(jnp.int32, (WIDTH, WIDTH), 1)
    apart = jnp.bitwise_xor(row, col)
    depth_of = jnp.where(row >= col, 0, -1)
    for bit in range(7):
        depth_of = depth_of + jnp.where((row > col) & (apart >= 2**bit), 1, 0)
    level[...] = depth_of

    pl.semaphore_wait(barrier, SIDE * SIDE - 1 + 4)

    rims = [
        pltpu.make_async_remote_copy(
            src_ref=source.at[pl.ds(WIDTH - 8, 8), :],
            dst_ref=rim.at[i],
            send_sem=rim_send.at[i],
            recv_sem=rim_recv.at[i],
            device_id=token_after,
            device_id_type=MESH,
        )
        for i, source in enumerate((query_hbm, key_hbm, value_hbm))
    ]
    for copy in rims:
        copy.start()
    for load in loads[:4]:
        load.wait()

    def weigh(values, lanes, which):
        total_sum = taps_ref[which, 3:4, lanes] * values
        for back in range(1, 4):
            total_sum += taps_ref[which, 3 - back : 4 - back, lanes] * pltpu.roll(values, back, 0)
        return total_sum

    def lay_down(count, lanes, sums, up, down, rate, end_row):
        rows = pl.ds(0, count)
        query, keys, values = [silu(s).astype(BF16).astype(F32) for s in sums]
        keys = keys * lax.rsqrt(jnp.sum(keys * keys, -1, keepdims=True) + 1e-06)
        falling = keys * down
        query_mid[rows, lanes] = (query * up).astype(BF16)
        key_mid[rows, lanes] = (rate * keys * up).astype(BF16)
        key_down[rows, lanes] = falling.astype(BF16)
        key_end[rows, lanes] = (falling * end_row).astype(BF16)
        value_rate[rows, lanes] = (rate * values).astype(BF16)

    def prepare(head, carry):
        lanes = lanes_of(head)
        lower = jnp.where(level[...] >= 0, 1.0, 0.0).astype(BF16)
        cumul = dot(lower, decay_in[:, lanes])
        middle = cumul[WIDTH // 2 - 1 : WIDTH // 2]
        last = cumul[WIDTH - 1 : WIDTH]
        up, down = jnp.exp(cumul - middle), jnp.exp(middle - cumul)
        end_row = jnp.exp(last - middle)
        pick = lax.broadcasted_iota(jnp.int32, (HEADS, WIDTH), 0) == head
        rate = dot(beta_ref[...], jnp.where(pick, 1.0, 0.0).astype(BF16))
        vectors[0:1, lanes] = jnp.exp(middle)
        vectors[1:2, lanes] = jnp.exp(last)
        vectors[2:3, lanes] = end_row
        edge[0, :, lanes] = up[:16]
        edge[1, :, lanes] = down[:16]
        edge[2, :, lanes] = rate[:16]
        sums = [
            weigh(source[:, lanes].astype(F32), lanes, i)
            for i, source in enumerate((query_in, key_in, value_in))
        ]
        lay_down(WIDTH, lanes, sums, up, down, rate, end_row)
        return carry

    lax.fori_loop(0, HEADS, prepare, 0)

    for copy in rims:
        copy.wait_recv()

    def mend(head, carry):
        lanes = lanes_of(head)
        sums = []
        for i, source in enumerate((query_in, key_in, value_in)):
            past = jnp.where(linear > 0, rim[i, :, lanes].astype(F32), 0.0)
            both = jnp.concatenate([past, source[0:16, lanes].astype(F32)], 0)
            sums.append(weigh(both, lanes, i)[8:])
        lay_down(
            16,
            lanes,
            sums,
            edge[0, :, lanes],
            edge[1, :, lanes],
            edge[2, :, lanes],
            vectors[2:3, lanes],
        )
        return carry

    lax.fori_loop(0, HEADS, mend, 0)

    def up_copy(slot, px, py):
        return pltpu.make_async_remote_copy(
            src_ref=send.at[slot],
            dst_ref=recv.at[place],
            send_sem=up_send.at[slot],
            recv_sem=up_recv.at[place],
            device_id=in_plane(px, py),
            device_id_type=MESH,
        )

    def group(turn, carry):
        py = lax.rem(y + (SIDE - 1) - turn, SIDE)
        columns = [lax.rem(x + dx, SIDE) for dx in range(SIDE)]
        heads = [py * SIDE + px for px in columns]
        lanes = [lanes_of(head) for head in heads]
        many = range(SIDE)
        depths = level[...]
        lower, scores, inverse = [], [], []
        for i in many:
            both = dot_nt(
                jnp.concatenate([key_mid[:, lanes[i]], query_mid[:, lanes[i]]], 0),
                key_down[:, lanes[i]],
            )
            lower.append(jnp.where(depths > 0, both[:WIDTH], 0.0).astype(BF16))
            scores.append(jnp.where(depths >= 0, both[WIDTH:], 0.0).astype(BF16))
        zero = jnp.zeros((WIDTH, WIDTH), BF16)
        one = jnp.where(depths == 0, 1.0, 0.0).astype(BF16)
        for i in many:
            inverse.append(one - jnp.where(depths == 1, lower[i], zero))
        for step in range(2, 8):
            parts = [dot(jnp.where(depths == step, lower[i], zero), inverse[i]) for i in many]
            parts = [dot(inverse[i], parts[i].astype(BF16)) for i in many]
            inverse = [inverse[i] - parts[i].astype(BF16) for i in many]
        for i in many:
            right = jnp.concatenate([value_rate[:, lanes[i]], key_mid[:, lanes[i]]], 1)
            solved = dot(inverse[i], right).astype(BF16)
            ends = dot_tn(key_end[:, lanes[i]], solved)
            insides = dot(scores[i], solved)
            mid_row = vectors[0:1, lanes[i]]
            fall_row = vectors[1:2, lanes[i]]
            diagonal = jnp.where(depths == 0, 1.0 - fall_row, 0.0)
            packed = jnp.concatenate(
                [ends[:, WIDTH:] * mid_row + diagonal, ends[:, :WIDTH]], 1
            ).astype(BF16)
            inner_out[heads[i]] = insides[:, :WIDTH]
            query_state[heads[i]] = (
                (query_mid[:, lanes[i]].astype(F32) - insides[:, WIDTH:]) * mid_row
            ).astype(BF16)
            slot = turn * SIDE + i
            if i == 0:

                @pl.when(turn == SIDE - 1)
                def _():
                    recv[place] = packed

                @pl.when(turn < SIDE - 1)
                def _():
                    send[slot] = packed
                    up_copy(slot, columns[0], py).start()
            else:
                send[slot] = packed
                up_copy(slot, columns[i], py).start()
        return carry

    lax.fori_loop(0, SIDE, group, 0)

    def await_up(source, carry):
        @pl.when(source != place)
        def _():
            pltpu.make_async_remote_copy(
                src_ref=send.at[0],
                dst_ref=recv.at[source],
                send_sem=up_send.at[0],
                recv_sem=up_recv.at[source],
                device_id=in_plane(x, y),
                device_id_type=MESH,
            ).wait_recv()

        return carry

    lax.fori_loop(0, HEADS, await_up, 0)

    for i in range(8):
        tree[i] = compose(recv[2 * i], recv[2 * i + 1]).astype(BF16)
    for i in range(4):
        tree[8 + i] = compose(tree[2 * i], tree[2 * i + 1]).astype(BF16)
    for i in range(2):
        tree[12 + i] = compose(tree[8 + 2 * i], tree[9 + 2 * i]).astype(BF16)
    tree[14] = compose(tree[12], tree[13]).astype(BF16)

    chain = pltpu.make_async_remote_copy(
        src_ref=state_out,
        dst_ref=state_in,
        send_sem=chain_send,
        recv_sem=chain_recv,
        device_id=z_after,
        device_id_type=MESH,
    )

    @pl.when(z == 0)
    def _():
        state_in[...] = jnp.zeros_like(state_in)

    @pl.when(z > 0)
    def _():
        chain.wait_recv()

    @pl.when(z < depth - 1)
    def _():
        state_out[...] = apply(tree[14], state_in[...]).astype(BF16)
        chain.start()

    begin = {0: state_in[...]}
    begin[8] = apply(tree[12], begin[0]).astype(BF16)
    for i in (0, 1):
        begin[8 * i + 4] = apply(tree[8 + 2 * i], begin[8 * i]).astype(BF16)
    for i in range(4):
        begin[4 * i + 2] = apply(tree[2 * i], begin[4 * i]).astype(BF16)
    for i in range(8):
        begin[2 * i + 1] = apply(recv[2 * i], begin[2 * i]).astype(BF16)
    for i in range(HEADS):
        starts[i] = begin[i]

    def down_copy(target):
        return pltpu.make_async_remote_copy(
            src_ref=starts.at[target],
            dst_ref=got.at[mine],
            send_sem=down_send.at[target],
            recv_sem=down_recv.at[mine],
            device_id=in_plane(lax.div(target, SIDE), lax.rem(target, SIDE)),
            device_id_type=MESH,
        )

    def hand_back(step, carry):
        target = lax.rem(place + 1 + step, HEADS)
        down_copy(target).start()
        return carry

    lax.fori_loop(0, HEADS - 1, hand_back, 0)
    got[mine] = starts[place]
    loads[4].wait()

    def conclude(step, carry):
        head = lax.rem(mine + HEADS - step, HEADS)

        @pl.when(step > 0)
        def _():
            pltpu.make_async_remote_copy(
                src_ref=starts.at[0],
                dst_ref=got.at[head],
                send_sem=down_send.at[0],
                recv_sem=down_recv.at[head],
                device_id=in_plane(x, y),
                device_id_type=MESH,
            ).wait_recv()

        lanes = lanes_of(head)
        attention = (inner_out[head] + dot(query_state[head], got[head])).astype(BF16).astype(F32)
        scale = lax.rsqrt(jnp.mean(attention * attention, -1, keepdims=True) + 1e-05)
        gate = 1.0 / (1.0 + jnp.exp(-gate_in[:, lanes].astype(F32)))
        out_ref[:, lanes] = (attention * scale * gain_ref[...] * gate).astype(BF16)
        return carry

    lax.fori_loop(0, HEADS, conclude, 0)

    for copy in rims:
        copy.wait_send()

    def settle_up(slot, carry):
        up_copy(slot, x, y).wait_send()
        return carry

    lax.fori_loop(0, SIDE * (SIDE - 1), settle_up, 0)
    lax.fori_loop(SIDE * (SIDE - 1) + 1, HEADS, settle_up, 0)

    def settle_down(target, carry):
        @pl.when(target != place)
        def _():
            down_copy(target).wait_send()

        return carry

    lax.fori_loop(0, HEADS, settle_down, 0)

    @pl.when(z < depth - 1)
    def _():
        chain.wait_send()


def layer(depth, query_raw, key_raw, value_raw, log_decay, beta, conv_weight, out_gate, norm_gain):
    rows, width = query_raw.shape
    wide = pltpu.VMEM((rows, width), BF16)
    dma = pltpu.SemaphoreType.DMA
    return pl.pallas_call(
        functools.partial(kernel, depth),
        out_shape=jax.ShapeDtypeStruct((rows, width), BF16),
        in_specs=[pl.BlockSpec(memory_space=pl.ANY)] * 5
        + [pl.BlockSpec(memory_space=pltpu.VMEM)] * 3,
        out_specs=pl.BlockSpec(memory_space=pltpu.VMEM),
        scratch_shapes=[wide] * 5
        + [pltpu.VMEM((3, 8, width), BF16)]
        + [wide] * 5
        + [
            pltpu.VMEM((3, 16, width), F32),
            pltpu.VMEM((8, width), F32),
            pltpu.VMEM((HEADS, WIDTH, WIDTH), F32),
            pltpu.VMEM((HEADS, WIDTH, WIDTH), BF16),
            pltpu.VMEM((WIDTH, WIDTH), jnp.int32),
            pltpu.VMEM((HEADS, WIDTH, 2 * WIDTH), BF16),
            pltpu.VMEM((HEADS, WIDTH, 2 * WIDTH), BF16),
            pltpu.VMEM((15, WIDTH, 2 * WIDTH), BF16),
            pltpu.VMEM((WIDTH, WIDTH), BF16),
            pltpu.VMEM((WIDTH, WIDTH), BF16),
            pltpu.VMEM((HEADS, WIDTH, WIDTH), BF16),
            pltpu.VMEM((HEADS, WIDTH, WIDTH), BF16),
            dma((5,)),
            dma((3,)),
            dma((3,)),
            dma((HEADS,)),
            dma((HEADS,)),
            dma,
            dma,
            dma((HEADS,)),
            dma((HEADS,)),
        ],
        compiler_params=pltpu.CompilerParams(
            collective_id=0, has_side_effects=True, vmem_limit_bytes=40 * 2**20
        ),
    )(
        query_raw,
        key_raw,
        value_raw,
        log_decay,
        out_gate,
        beta,
        conv_weight,
        norm_gain.reshape(1, WIDTH),
    )


def solution(mesh):
    tokens = P(("dp", "ctx", "head"), None)
    return jax.shard_map(
        functools.partial(layer, mesh.shape["ctx"] // SIDE),
        mesh=mesh,
        in_specs=(tokens, tokens, tokens, tokens, tokens, P(), tokens, P()),
        out_specs=tokens,
        check_vma=False,
    )
```

```python
import functools

import jax
import jax.numpy as jnp
from jax import lax
from jax.experimental import pallas as pl
from jax.experimental.pallas import tpu as pltpu
from jax.sharding import PartitionSpec as P

MESH = pl.DeviceIdType.MESH
WIDTH = 128
HEADS = 16
SIDE = 4
F32 = jnp.float32
BF16 = jnp.bfloat16


def dot(a, b):
    return jnp.dot(a, b, preferred_element_type=F32)


def dot_nt(a, b):
    return lax.dot_general(a, b, (((1,), (1,)), ((), ())), preferred_element_type=F32)


def dot_tn(a, b):
    return lax.dot_general(a, b, (((0,), (0,)), ((), ())), preferred_element_type=F32)


TURNS = (
    ((2, 2), (2, 1), (1, 2), (3, 3)),
    ((2, 3), (3, 2), (1, 1), (0, 3)),
    ((1, 3), (3, 1), (2, 0), (0, 2)),
    ((0, 0), (1, 0), (3, 0), (0, 1)),
)


def pick(turn, choices):
    value = choices[-1]
    for i in range(len(choices) - 1):
        value = jnp.where(turn == i, choices[i], value)
    return value


def lanes_of(index):
    return pl.ds(pl.multiple_of(index * WIDTH, WIDTH), WIDTH)


def silu(u):
    return u / (1.0 + jnp.exp(-u))


def compose(first, second):
    return first.astype(F32) - dot(second[:, :WIDTH], first) + second.astype(F32)


def apply(step, state):
    return state.astype(F32) - dot(step[:, :WIDTH], state) + step[:, WIDTH:].astype(F32)


def kernel(
    depth,
    query_hbm,
    key_hbm,
    value_hbm,
    decay_hbm,
    gate_hbm,
    beta_hbm,
    taps_hbm,
    gain_hbm,
    out_ref,
    query_in,
    key_in,
    value_in,
    decay_in,
    gate_in,
    beta_ref,
    taps_ref,
    gain_ref,
    rim,
    query_mid,
    key_mid,
    key_down,
    key_end,
    value_rate,
    edge,
    vectors,
    inner_out,
    query_state,
    level,
    scores_kept,
    solved_kept,
    gates,
    send,
    recv,
    tree,
    behind,
    near,
    state_in,
    state_out,
    begins,
    starts,
    got,
    load_sem,
    rim_send,
    rim_recv,
    up_send,
    up_recv,
    pair_send,
    pair_recv,
    near_send,
    near_recv,
    state_send,
    state_recv,
    down_send,
    down_recv,
):
    ctx, y = lax.axis_index("ctx"), lax.axis_index("head")
    x, z = lax.rem(ctx, SIDE), lax.div(ctx, SIDE)
    place = x * SIDE + y
    mine = y * SIDE + x
    total = depth * SIDE * SIDE
    linear = ctx * SIDE + y
    after = lax.rem(linear + 1, total)
    before = lax.rem(linear + total - 1, total)

    def device(cx, cy):
        return {"ctx": cx, "head": cy}

    def in_plane(px, py):
        return device(z * SIDE + px, py)

    def in_line(ahead):
        return device(lax.rem(z + ahead, depth) * SIDE + x, y)

    token_after = device(lax.div(after, SIDE), lax.rem(after, SIDE))
    token_before = device(lax.div(before, SIDE), lax.rem(before, SIDE))

    barrier = pltpu.get_barrier_semaphore()
    for dx in range(SIDE):
        for dy in range(SIDE):
            if dx or dy:
                pl.semaphore_signal(
                    barrier,
                    inc=1,
                    device_id=in_plane(lax.rem(x + dx, SIDE), lax.rem(y + dy, SIDE)),
                    device_id_type=MESH,
                )
    for other in [in_line(ahead) for ahead in range(1, depth)] + [token_after, token_before]:
        pl.semaphore_signal(barrier, inc=1, device_id=other, device_id_type=MESH)

    loads = [
        pltpu.make_async_copy(source, target, load_sem.at[i])
        for i, (source, target) in enumerate(
            (
                (decay_hbm, decay_in),
                (beta_hbm, beta_ref),
                (taps_hbm, taps_ref),
                (query_hbm, query_in),
                (key_hbm, key_in),
                (value_hbm, value_in),
                (gate_hbm, gate_in),
                (gain_hbm, gain_ref),
            )
        )
    ]
    for load in loads:
        load.start()

    row = lax.broadcasted_iota(jnp.int32, (WIDTH, WIDTH), 0)
    col = lax.broadcasted_iota(jnp.int32, (WIDTH, WIDTH), 1)
    apart = jnp.bitwise_xor(row, col)
    depth_of = jnp.where(row >= col, 0, -1)
    for bit in range(7):
        depth_of = depth_of + jnp.where((row > col) & (apart >= 2**bit), 1, 0)
    level[...] = depth_of

    pl.semaphore_wait(barrier, SIDE * SIDE - 1 + depth - 1 + 2)

    rims = [
        pltpu.make_async_remote_copy(
            src_ref=source.at[pl.ds(WIDTH - 8, 8), :],
            dst_ref=rim.at[i],
            send_sem=rim_send.at[i],
            recv_sem=rim_recv.at[i],
            device_id=token_after,
            device_id_type=MESH,
        )
        for i, source in enumerate((query_hbm, key_hbm, value_hbm))
    ]
    for copy in rims:
        copy.start()
    for load in loads[:6]:
        load.wait()

    def weigh(values, lanes, which):
        total_sum = taps_ref[which, 3:4, lanes] * values
        for back in range(1, 4):
            total_sum += taps_ref[which, 3 - back : 4 - back, lanes] * pltpu.roll(values, back, 0)
        return total_sum

    def lay_down(count, lanes, sums, up, down, rate, end_row):
        rows = pl.ds(0, count)
        query, keys, values = [silu(s).astype(BF16).astype(F32) for s in sums]
        keys = keys * lax.rsqrt(jnp.sum(keys * keys, -1, keepdims=True) + 1e-06)
        falling = keys * down
        query_mid[rows, lanes] = (query * up).astype(BF16)
        key_mid[rows, lanes] = (rate * keys * up).astype(BF16)
        key_down[rows, lanes] = falling.astype(BF16)
        key_end[rows, lanes] = (falling * end_row).astype(BF16)
        value_rate[rows, lanes] = (rate * values).astype(BF16)

    def prepare(head, carry):
        lanes = lanes_of(head)
        lower = jnp.where(level[...] >= 0, 1.0, 0.0).astype(BF16)
        cumul = dot(lower, decay_in[:, lanes])
        middle = cumul[WIDTH // 2 - 1 : WIDTH // 2]
        last = cumul[WIDTH - 1 : WIDTH]
        up, down = jnp.exp(cumul - middle), jnp.exp(middle - cumul)
        end_row = jnp.exp(last - middle)
        chosen = lax.broadcasted_iota(jnp.int32, (HEADS, WIDTH), 0) == head
        rate = dot_tn(beta_ref[...], jnp.where(chosen, 1.0, 0.0).astype(BF16))
        vectors[0:1, lanes] = jnp.exp(middle)
        vectors[1:2, lanes] = jnp.exp(last)
        vectors[2:3, lanes] = end_row
        edge[0, :, lanes] = up[:16]
        edge[1, :, lanes] = down[:16]
        edge[2, :, lanes] = rate[:16]
        sums = [
            weigh(source[:, lanes].astype(F32), lanes, i)
            for i, source in enumerate((query_in, key_in, value_in))
        ]
        lay_down(WIDTH, lanes, sums, up, down, rate, end_row)
        return carry

    lax.fori_loop(0, HEADS, prepare, 0, unroll=2)

    for copy in rims:
        copy.wait_recv()

    def mend(head, carry):
        lanes = lanes_of(head)
        sums = []
        for i, source in enumerate((query_in, key_in, value_in)):
            past = jnp.where(linear > 0, rim[i, :, lanes].astype(F32), 0.0)
            both = jnp.concatenate([past, source[0:16, lanes].astype(F32)], 0)
            sums.append(weigh(both, lanes, i)[8:])
        lay_down(
            16,
            lanes,
            sums,
            edge[0, :, lanes],
            edge[1, :, lanes],
            edge[2, :, lanes],
            vectors[2:3, lanes],
        )
        return carry

    lax.fori_loop(0, HEADS, mend, 0, unroll=4)

    def up_copy(slot, px, py):
        return pltpu.make_async_remote_copy(
            src_ref=send.at[slot],
            dst_ref=recv.at[place],
            send_sem=up_send.at[slot],
            recv_sem=up_recv.at[place],
            device_id=in_plane(px, py),
            device_id_type=MESH,
        )

    def group(turn, carry):
        spots = [[pick(turn, [t[i][axis] for t in TURNS]) for axis in (0, 1)] for i in range(SIDE)]
        spots = [(lax.rem(x + dx, SIDE), lax.rem(y + dy, SIDE)) for dx, dy in spots]
        heads = [py * SIDE + px for px, py in spots]
        lanes = [lanes_of(head) for head in heads]
        many = range(SIDE)
        depths = level[...]
        lower, inverse = [], []
        for i in many:
            both = dot_nt(
                jnp.concatenate([key_mid[:, lanes[i]], query_mid[:, lanes[i]]], 0),
                key_down[:, lanes[i]],
            )
            lower.append(jnp.where(depths > 0, both[:WIDTH], 0.0).astype(BF16))
            scores_kept[heads[i]] = jnp.where(depths >= 0, both[WIDTH:], 0.0).astype(BF16)
        zero = jnp.zeros((WIDTH, WIDTH), BF16)
        one = jnp.where(depths == 0, 1.0, 0.0).astype(BF16)
        for i in many:
            inverse.append(one - jnp.where(depths == 1, lower[i], zero))
        for step in range(2, 8):
            parts = [dot(jnp.where(depths == step, lower[i], zero), inverse[i]) for i in many]
            parts = [dot(inverse[i], parts[i].astype(BF16)) for i in many]
            inverse = [inverse[i] - parts[i].astype(BF16) for i in many]
        for i in many:
            right = jnp.concatenate([value_rate[:, lanes[i]], key_mid[:, lanes[i]]], 1)
            solved = dot(inverse[i], right).astype(BF16)
            ends = dot_tn(key_end[:, lanes[i]], solved)
            solved_kept[heads[i]] = solved
            mid_row = vectors[0:1, lanes[i]]
            fall_row = vectors[1:2, lanes[i]]
            diagonal = jnp.where(depths == 0, 1.0 - fall_row, 0.0)
            packed = jnp.concatenate(
                [ends[:, WIDTH:] * mid_row + diagonal, ends[:, :WIDTH]], 1
            ).astype(BF16)
            slot = turn * SIDE + i
            if i == 0:

                @pl.when(turn == SIDE - 1)
                def _():
                    recv[place] = packed

                @pl.when(turn < SIDE - 1)
                def _():
                    send[slot] = packed
                    up_copy(slot, *spots[0]).start()
            else:
                send[slot] = packed
                up_copy(slot, *spots[i]).start()
        return carry

    lax.fori_loop(0, SIDE, group, 0)

    def await_up(source, carry):
        @pl.when(source != place)
        def _():
            pltpu.make_async_remote_copy(
                src_ref=send.at[0],
                dst_ref=recv.at[source],
                send_sem=up_send.at[0],
                recv_sem=up_recv.at[source],
                device_id=in_plane(x, y),
                device_id_type=MESH,
            ).wait_recv()

        return carry

    lax.fori_loop(0, HEADS, await_up, 0)

    for i in range(8):
        tree[i] = compose(recv[2 * i], recv[2 * i + 1]).astype(BF16)
    for i in range(4):
        tree[8 + i] = compose(tree[2 * i], tree[2 * i + 1]).astype(BF16)
    for i in range(2):
        tree[12 + i] = compose(tree[8 + 2 * i], tree[9 + 2 * i]).astype(BF16)
    tree[14] = compose(tree[12], tree[13]).astype(BF16)

    def inside(head, carry):
        lanes = lanes_of(head)
        inner = dot(scores_kept[head], solved_kept[head])
        inner_out[head] = inner[:, :WIDTH]
        query_state[head] = (
            (query_mid[:, lanes].astype(F32) - inner[:, WIDTH:]) * vectors[0:1, lanes]
        ).astype(BF16)
        gate = 1.0 / (1.0 + jnp.exp(-gate_in[:, lanes].astype(F32)))
        gates[head] = gain_ref[...] * gate
        return carry

    for load in loads[6:]:
        load.wait()

    def z_copy(source, target, sent, landed, ahead):
        return pltpu.make_async_remote_copy(
            src_ref=source,
            dst_ref=target,
            send_sem=sent,
            recv_sem=landed,
            device_id=in_line(ahead),
            device_id_type=MESH,
        )

    def pair_copy(source, ahead):
        return z_copy(source, behind, pair_send.at[ahead - 1], pair_recv, ahead)

    def state_copy(ahead):
        return z_copy(state_out, state_in, state_send.at[ahead - 1], state_recv, ahead)

    whole = tree.at[14]
    near_copy = z_copy(whole, near, near_send, near_recv, 1)

    @pl.when((z == 2) | (z == 4))
    def _():
        pair_copy(whole, 1).start()

    @pl.when(z == 6)
    def _():
        near_copy.start()

    @pl.when(z == 0)
    def _():
        state_out[...] = tree[14, :, WIDTH:]
        state_copy(1).start()
        begins[...] = jnp.zeros_like(begins)

    @pl.when(z >= 4)
    def _():
        lax.fori_loop(0, HEADS, inside, 0, unroll=4)

    @pl.when((z == 3) | (z >= 5))
    def _():
        pair_copy(whole, 1).wait_recv()

    @pl.when((z == 3) | (z == 5))
    def _():
        tree[15] = compose(behind[...], tree[14]).astype(BF16)

    @pl.when(z == 5)
    def _():
        pair_copy(tree.at[15], 2).start()
        pair_copy(tree.at[15], 1).start()

    @pl.when(z == 7)
    def _():
        near_copy.wait_recv()

    @pl.when(z > 0)
    def _():
        state_copy(1).wait_recv()

    @pl.when(z == 1)
    def _():
        state_out[...] = apply(tree[14], state_in[...]).astype(BF16)
        state_copy(2).start()
        state_copy(1).start()

    @pl.when(z == 3)
    def _():
        state_out[...] = apply(tree[15], state_in[...]).astype(BF16)
        for ahead in (4, 3, 2, 1):
            state_copy(ahead).start()

    @pl.when((z == 1) | (z == 2) | (z == 4))
    def _():
        begins[...] = state_in[...]

    @pl.when((z == 3) | (z >= 5))
    def _():
        begins[...] = apply(behind[...], state_in[...]).astype(BF16)

    @pl.when(z == 7)
    def _():
        begins[...] = apply(near[...], begins[...]).astype(BF16)

    begin = {0: begins[...]}
    begin[8] = apply(tree[12], begin[0]).astype(BF16)
    for i in (0, 1):
        begin[8 * i + 4] = apply(tree[8 + 2 * i], begin[8 * i]).astype(BF16)
    for i in range(4):
        begin[4 * i + 2] = apply(tree[2 * i], begin[4 * i]).astype(BF16)
    for i in range(8):
        begin[2 * i + 1] = apply(recv[2 * i], begin[2 * i]).astype(BF16)
    for i in range(HEADS):
        starts[i] = begin[i]

    offsets = [spot for turn in TURNS for spot in turn if spot != (0, 0)]

    def down_copy(step):
        dx, dy = offsets[step]
        px, py = lax.rem(x + dx, SIDE), lax.rem(y + dy, SIDE)
        return pltpu.make_async_remote_copy(
            src_ref=starts.at[px * SIDE + py],
            dst_ref=got.at[mine],
            send_sem=down_send.at[step],
            recv_sem=down_recv.at[mine],
            device_id=in_plane(px, py),
            device_id_type=MESH,
        )

    for step in range(HEADS - 1):
        down_copy(step).start()
    got[mine] = starts[place]

    @pl.when(z < 4)
    def _():
        lax.fori_loop(0, HEADS, inside, 0, unroll=4)

    def await_down(head):
        pltpu.make_async_remote_copy(
            src_ref=starts.at[0],
            dst_ref=got.at[head],
            send_sem=down_send.at[0],
            recv_sem=down_recv.at[head],
            device_id=in_plane(x, y),
            device_id_type=MESH,
        ).wait_recv()

    owners = [mine]
    for dx, dy in offsets:
        owners.append(lax.rem(y + SIDE - dy, SIDE) * SIDE + lax.rem(x + SIDE - dx, SIDE))
    for part in range(SIDE):
        now = owners[SIDE * part : SIDE * part + SIDE]
        for step, head in enumerate(now):
            if part or step:
                await_down(head)
        for head in now:
            attention = inner_out[head] + dot(query_state[head], got[head])
            attention = attention.astype(BF16).astype(F32)
            scale = lax.rsqrt(jnp.mean(attention * attention, -1, keepdims=True) + 1e-05)
            out_ref[:, lanes_of(head)] = (attention * scale * gates[head]).astype(BF16)

    for copy in rims:
        copy.wait_send()

    def settle_up(slot, carry):
        up_copy(slot, x, y).wait_send()
        return carry

    lax.fori_loop(0, SIDE * (SIDE - 1), settle_up, 0)
    lax.fori_loop(SIDE * (SIDE - 1) + 1, HEADS, settle_up, 0)
    for step in range(HEADS - 1):
        down_copy(step).wait_send()

    @pl.when((z == 2) | (z == 4) | (z == 5))
    def _():
        pair_copy(whole, 1).wait_send()

    @pl.when(z == 5)
    def _():
        pair_copy(whole, 2).wait_send()

    @pl.when(z == 6)
    def _():
        near_copy.wait_send()

    @pl.when((z == 0) | (z == 1) | (z == 3))
    def _():
        state_copy(1).wait_send()

    @pl.when((z == 1) | (z == 3))
    def _():
        state_copy(2).wait_send()

    @pl.when(z == 3)
    def _():
        state_copy(3).wait_send()
        state_copy(4).wait_send()


def layer(depth, query_raw, key_raw, value_raw, log_decay, beta, conv_weight, out_gate, norm_gain):
    rows, width = query_raw.shape
    wide = pltpu.VMEM((rows, width), BF16)
    dma = pltpu.SemaphoreType.DMA
    return pl.pallas_call(
        functools.partial(kernel, depth),
        out_shape=jax.ShapeDtypeStruct((rows, width), BF16),
        in_specs=[pl.BlockSpec(memory_space=pltpu.HBM)] * 8,
        out_specs=pl.BlockSpec(memory_space=pltpu.VMEM),
        scratch_shapes=[wide] * 5
        + [
            pltpu.VMEM(beta.shape[::-1], BF16),
            pltpu.VMEM(conv_weight.shape, F32),
            pltpu.VMEM((1, WIDTH), F32),
            pltpu.VMEM((3, 8, width), BF16),
        ]
        + [wide] * 5
        + [
            pltpu.VMEM((3, 16, width), F32),
            pltpu.VMEM((8, width), F32),
            pltpu.VMEM((HEADS, WIDTH, WIDTH), F32),
            pltpu.VMEM((HEADS, WIDTH, WIDTH), BF16),
            pltpu.VMEM((WIDTH, WIDTH), jnp.int32),
            pltpu.VMEM((HEADS, WIDTH, WIDTH), BF16),
            pltpu.VMEM((HEADS, WIDTH, 2 * WIDTH), BF16),
            pltpu.VMEM((HEADS, WIDTH, WIDTH), F32),
            pltpu.VMEM((HEADS, WIDTH, 2 * WIDTH), BF16),
            pltpu.VMEM((HEADS, WIDTH, 2 * WIDTH), BF16),
            pltpu.VMEM((16, WIDTH, 2 * WIDTH), BF16),
            pltpu.VMEM((WIDTH, 2 * WIDTH), BF16),
            pltpu.VMEM((WIDTH, 2 * WIDTH), BF16),
            pltpu.VMEM((WIDTH, WIDTH), BF16),
            pltpu.VMEM((WIDTH, WIDTH), BF16),
            pltpu.VMEM((WIDTH, WIDTH), BF16),
            pltpu.VMEM((HEADS, WIDTH, WIDTH), BF16),
            pltpu.VMEM((HEADS, WIDTH, WIDTH), BF16),
            dma((8,)),
            dma((3,)),
            dma((3,)),
            dma((HEADS,)),
            dma((HEADS,)),
            dma((2,)),
            dma,
            dma,
            dma,
            dma((4,)),
            dma,
            dma((HEADS,)),
            dma((HEADS,)),
        ],
        compiler_params=pltpu.CompilerParams(
            collective_id=0, has_side_effects=True, vmem_limit_bytes=40 * 2**20
        ),
    )(
        *[
            pltpu.with_memory_space_constraint(array, pltpu.HBM)
            for array in (
                query_raw,
                key_raw,
                value_raw,
                log_decay,
                out_gate,
                beta.T,
                conv_weight,
                norm_gain.reshape(1, WIDTH),
            )
        ]
    )


def solution(mesh):
    tokens = P(("dp", "ctx", "head"), None)
    return jax.shard_map(
        functools.partial(layer, mesh.shape["ctx"] // SIDE),
        mesh=mesh,
        in_specs=(tokens, tokens, tokens, tokens, tokens, P(), tokens, P()),
        out_specs=tokens,
        check_vma=False,
    )
```

```python
import functools

import jax
import jax.numpy as jnp
from jax import lax
from jax.experimental import pallas as pl
from jax.experimental.pallas import tpu as pltpu
from jax.sharding import PartitionSpec as P

MESH = pl.DeviceIdType.MESH
WIDTH = 128
HEADS = 16
SIDE = 4
F32 = jnp.float32
BF16 = jnp.bfloat16


def dot(a, b):
    return jnp.dot(a, b, preferred_element_type=F32)


def dot_nt(a, b):
    return lax.dot_general(a, b, (((1,), (1,)), ((), ())), preferred_element_type=F32)


def dot_tn(a, b):
    return lax.dot_general(a, b, (((0,), (0,)), ((), ())), preferred_element_type=F32)


OFFSETS = (
    ((2, 2), (2, 1), (1, 2), (3, 3))
    + ((2, 3), (3, 2), (1, 1), (0, 3))
    + ((1, 3), (3, 1), (2, 0), (0, 2))
    + ((1, 0), (3, 0), (0, 1), (0, 0))
)


def entry(position, table):
    if len(table) == 1:
        return table[0]
    half = lax.div(position, 2)
    odd = lax.rem(position, 2) == 1
    return jnp.where(odd, entry(half, table[1::2]), entry(half, table[::2]))


def lanes_of(index):
    return pl.ds(pl.multiple_of(index * WIDTH, WIDTH), WIDTH)


def silu(u):
    return u / (1.0 + jnp.exp(-u))


def compose(first, second):
    return first.astype(F32) - dot(second[:, :WIDTH], first) + second.astype(F32)


def apply(step, state):
    return state.astype(F32) - dot(step[:, :WIDTH], state) + step[:, WIDTH:].astype(F32)


def kernel(
    depth,
    query_hbm,
    key_hbm,
    value_hbm,
    decay_hbm,
    gate_hbm,
    beta_hbm,
    taps_hbm,
    gain_hbm,
    out_ref,
    query_in,
    key_in,
    value_in,
    decay_in,
    gate_in,
    beta_ref,
    taps_ref,
    gain_ref,
    rim,
    query_mid,
    key_mid,
    key_down,
    key_end,
    value_rate,
    edge,
    vectors,
    inner_out,
    query_state,
    level,
    scores_kept,
    solved_kept,
    gates,
    send,
    recv,
    tree,
    behind,
    near,
    state_in,
    state_out,
    begins,
    starts,
    got,
    load_sem,
    rim_send,
    rim_recv,
    up_send,
    up_recv,
    pair_send,
    pair_recv,
    near_send,
    near_recv,
    state_send,
    state_recv,
    down_send,
    down_recv,
):
    ctx, y = lax.axis_index("ctx"), lax.axis_index("head")
    x, z = lax.rem(ctx, SIDE), lax.div(ctx, SIDE)
    place = x * SIDE + y
    mine = y * SIDE + x
    total = depth * SIDE * SIDE
    linear = ctx * SIDE + y
    after = lax.rem(linear + 1, total)
    before = lax.rem(linear + total - 1, total)

    def device(cx, cy):
        return {"ctx": cx, "head": cy}

    def in_plane(px, py):
        return device(z * SIDE + px, py)

    def in_line(ahead):
        return device(lax.rem(z + ahead, depth) * SIDE + x, y)

    token_after = device(lax.div(after, SIDE), lax.rem(after, SIDE))
    token_before = device(lax.div(before, SIDE), lax.rem(before, SIDE))

    barrier = pltpu.get_barrier_semaphore()
    for dx in range(SIDE):
        for dy in range(SIDE):
            if dx or dy:
                pl.semaphore_signal(
                    barrier,
                    inc=1,
                    device_id=in_plane(lax.rem(x + dx, SIDE), lax.rem(y + dy, SIDE)),
                    device_id_type=MESH,
                )
    for other in [in_line(ahead) for ahead in range(1, depth)] + [token_after, token_before]:
        pl.semaphore_signal(barrier, inc=1, device_id=other, device_id_type=MESH)

    loads = [
        pltpu.make_async_copy(source, target, load_sem.at[i])
        for i, (source, target) in enumerate(
            (
                (decay_hbm, decay_in),
                (beta_hbm, beta_ref),
                (taps_hbm, taps_ref),
                (query_hbm, query_in),
                (key_hbm, key_in),
                (value_hbm, value_in),
                (gate_hbm, gate_in),
                (gain_hbm, gain_ref),
            )
        )
    ]
    for load in loads:
        load.start()

    row = lax.broadcasted_iota(jnp.int32, (WIDTH, WIDTH), 0)
    col = lax.broadcasted_iota(jnp.int32, (WIDTH, WIDTH), 1)
    apart = jnp.bitwise_xor(row, col)
    depth_of = jnp.where(row >= col, 0, -1)
    for bit in range(7):
        depth_of = depth_of + jnp.where((row > col) & (apart >= 2**bit), 1, 0)
    level[...] = depth_of

    pl.semaphore_wait(barrier, SIDE * SIDE - 1 + depth - 1 + 2)

    rims = [
        pltpu.make_async_remote_copy(
            src_ref=source.at[pl.ds(WIDTH - 8, 8), :],
            dst_ref=rim.at[i],
            send_sem=rim_send.at[i],
            recv_sem=rim_recv.at[i],
            device_id=token_after,
            device_id_type=MESH,
        )
        for i, source in enumerate((query_hbm, key_hbm, value_hbm))
    ]
    for copy in rims:
        copy.start()
    for load in loads[:6]:
        load.wait()

    def weigh(values, lanes, which):
        total_sum = taps_ref[which, 3:4, lanes] * values
        for back in range(1, 4):
            total_sum += taps_ref[which, 3 - back : 4 - back, lanes] * pltpu.roll(values, back, 0)
        return total_sum

    def lay_down(count, lanes, sums, up, down, rate, end_row):
        rows = pl.ds(0, count)
        query, keys, values = [silu(s).astype(BF16).astype(F32) for s in sums]
        keys = keys * lax.rsqrt(jnp.sum(keys * keys, -1, keepdims=True) + 1e-06)
        falling = keys * down
        query_mid[rows, lanes] = (query * up).astype(BF16)
        key_mid[rows, lanes] = (rate * keys * up).astype(BF16)
        key_down[rows, lanes] = falling.astype(BF16)
        key_end[rows, lanes] = (falling * end_row).astype(BF16)
        value_rate[rows, lanes] = (rate * values).astype(BF16)

    def spot_at(position):
        if isinstance(position, int):
            dx, dy = OFFSETS[position]
        else:
            dx, dy = [entry(position, [offset[axis] for offset in OFFSETS]) for axis in (0, 1)]
        return lax.rem(x + dx, SIDE), lax.rem(y + dy, SIDE)

    def head_at(position):
        px, py = spot_at(position)
        return py * SIDE + px

    def prepare(position, carry):
        head = head_at(position)
        lanes = lanes_of(head)
        lower = jnp.where(level[...] >= 0, 1.0, 0.0).astype(BF16)
        cumul = dot(lower, decay_in[:, lanes])
        middle = cumul[WIDTH // 2 - 1 : WIDTH // 2]
        last = cumul[WIDTH - 1 : WIDTH]
        up, down = jnp.exp(cumul - middle), jnp.exp(middle - cumul)
        end_row = jnp.exp(last - middle)
        chosen = lax.broadcasted_iota(jnp.int32, (HEADS, WIDTH), 0) == head
        rate = dot_tn(beta_ref[...], jnp.where(chosen, 1.0, 0.0).astype(BF16))
        vectors[0:1, lanes] = jnp.exp(middle)
        vectors[1:2, lanes] = jnp.exp(last)
        vectors[2:3, lanes] = end_row
        edge[0, :, lanes] = up[:16]
        edge[1, :, lanes] = down[:16]
        edge[2, :, lanes] = rate[:16]
        sums = [
            weigh(source[:, lanes].astype(F32), lanes, i)
            for i, source in enumerate((query_in, key_in, value_in))
        ]
        lay_down(WIDTH, lanes, sums, up, down, rate, end_row)
        return carry

    lax.fori_loop(0, 8, prepare, 0, unroll=2)

    for copy in rims:
        copy.wait_recv()

    def mend(position):
        lanes = lanes_of(head_at(position))
        sums = []
        for i, source in enumerate((query_in, key_in, value_in)):
            past = jnp.where(linear > 0, rim[i, :, lanes].astype(F32), 0.0)
            both = jnp.concatenate([past, source[0:16, lanes].astype(F32)], 0)
            sums.append(weigh(both, lanes, i)[8:])
        lay_down(
            16,
            lanes,
            sums,
            edge[0, :, lanes],
            edge[1, :, lanes],
            edge[2, :, lanes],
            vectors[2:3, lanes],
        )

    def up_copy(slot, px, py):
        return pltpu.make_async_remote_copy(
            src_ref=send.at[slot],
            dst_ref=recv.at[place],
            send_sem=up_send.at[slot],
            recv_sem=up_recv.at[place],
            device_id=in_plane(px, py),
            device_id_type=MESH,
        )

    def group(positions):
        for position in positions:
            mend(position)
        spots = [spot_at(position) for position in positions]
        heads = [py * SIDE + px for px, py in spots]
        lanes = [lanes_of(head) for head in heads]
        many = range(len(positions))
        depths = level[...]
        zero = jnp.zeros((WIDTH, WIDTH), BF16)
        one = jnp.where(depths == 0, 1.0, 0.0).astype(BF16)
        lower, rest, inverse, right, solved = [], [], [], [], []
        for i in many:
            both = dot_nt(
                jnp.concatenate([key_mid[:, lanes[i]], query_mid[:, lanes[i]]], 0),
                key_down[:, lanes[i]],
            )
            exact = jnp.where(depths > 0, both[:WIDTH], 0.0)
            lower.append(exact.astype(BF16))
            rest.append((exact - lower[i].astype(F32)).astype(BF16))
            scores_kept[heads[i]] = jnp.where(depths >= 0, both[WIDTH:], 0.0).astype(BF16)
            inverse.append(one - jnp.where(depths == 1, lower[i], zero))
            right.append(jnp.concatenate([value_rate[:, lanes[i]], key_mid[:, lanes[i]]], 1))
        guess = []
        for step in (2, 4, 6):
            near_part = (depths == step) | (depths == step + 1)
            fall = [jnp.where(near_part, lower[i], zero) for i in many]
            if step == 6:
                fall = [jnp.concatenate([fall[i], right[i]], 1) for i in many]
            parts = [dot(inverse[i], fall[i]) for i in many]
            bases = [inverse[i].astype(F32) for i in many]
            if step == 6:
                bases = [jnp.concatenate([bases[i], parts[i][:, WIDTH:]], 1) for i in many]
            parts = [parts[i][:, :WIDTH].astype(BF16) for i in many]
            twice = [
                dot(parts[i], jnp.concatenate([parts[i], bases[i].astype(BF16)], 1)) for i in many
            ]
            halves = [bases[i] - twice[i][:, WIDTH:] for i in many]
            halves = [
                halves[i] + dot(twice[i][:, :WIDTH].astype(BF16), halves[i].astype(BF16))
                for i in many
            ]
            inverse = [halves[i][:, :WIDTH].astype(BF16) for i in many]
            if step == 6:
                guess = [halves[i][:, WIDTH:].astype(BF16) for i in many]
        miss = [
            right[i].astype(F32)
            - guess[i].astype(F32)
            - dot(
                jnp.concatenate([lower[i], rest[i]], 1), jnp.concatenate([guess[i], guess[i]], 0)
            )
            for i in many
        ]
        solved = [
            (guess[i].astype(F32) + dot(inverse[i], miss[i].astype(BF16))).astype(BF16)
            for i in many
        ]
        for i in many:
            ends = dot_tn(key_end[:, lanes[i]], solved[i])
            solved_kept[heads[i]] = solved[i]
            mid_row = vectors[0:1, lanes[i]]
            fall_row = vectors[1:2, lanes[i]]
            diagonal = jnp.where(depths == 0, 1.0 - fall_row, 0.0)
            packed = jnp.concatenate(
                [ends[:, WIDTH:] * mid_row + diagonal, ends[:, :WIDTH]], 1
            ).astype(BF16)
            slot = positions[i]

            def leave(slot=slot, packed=packed, i=i):
                send[slot] = packed
                up_copy(slot, *spots[i]).start()

            def keep(packed=packed):
                recv[place] = packed

            if i == SIDE - 1:
                pl.when(slot < HEADS - 1)(leave)
                pl.when(slot == HEADS - 1)(keep)
            else:
                leave()

    def turns(turn, carry):
        group([SIDE * turn + i for i in range(SIDE)])

        @pl.when((turn == 1) | (turn == 2))
        def _():
            lax.fori_loop(0, SIDE, lambda i, c: prepare(SIDE * turn + SIDE + i, c), 0, unroll=2)

        return carry

    lax.fori_loop(0, SIDE, turns, 0)

    def await_up(source, carry):
        @pl.when(source != place)
        def _():
            pltpu.make_async_remote_copy(
                src_ref=send.at[0],
                dst_ref=recv.at[source],
                send_sem=up_send.at[0],
                recv_sem=up_recv.at[source],
                device_id=in_plane(x, y),
                device_id_type=MESH,
            ).wait_recv()

        return carry

    lax.fori_loop(0, HEADS, await_up, 0)

    for i in range(8):
        tree[i] = compose(recv[2 * i], recv[2 * i + 1]).astype(BF16)
    for i in range(4):
        tree[8 + i] = compose(tree[2 * i], tree[2 * i + 1]).astype(BF16)
    for i in range(2):
        tree[12 + i] = compose(tree[8 + 2 * i], tree[9 + 2 * i]).astype(BF16)
    tree[14] = compose(tree[12], tree[13]).astype(BF16)

    def inside(head, carry):
        lanes = lanes_of(head)
        inner = dot(scores_kept[head], solved_kept[head])
        inner_out[head] = inner[:, :WIDTH]
        query_state[head] = (
            (query_mid[:, lanes].astype(F32) - inner[:, WIDTH:]) * vectors[0:1, lanes]
        ).astype(BF16)
        gate = 1.0 / (1.0 + jnp.exp(-gate_in[:, lanes].astype(F32)))
        gates[head] = gain_ref[...] * gate
        return carry

    for load in loads[6:]:
        load.wait()

    def z_copy(source, target, sent, landed, ahead):
        return pltpu.make_async_remote_copy(
            src_ref=source,
            dst_ref=target,
            send_sem=sent,
            recv_sem=landed,
            device_id=in_line(ahead),
            device_id_type=MESH,
        )

    def pair_copy(source, ahead):
        return z_copy(source, behind, pair_send.at[ahead - 1], pair_recv, ahead)

    def state_copy(ahead):
        return z_copy(state_out, state_in, state_send.at[ahead - 1], state_recv, ahead)

    whole = tree.at[14]
    near_copy = z_copy(whole, near, near_send, near_recv, jnp.where(z == 1, 2, 1))

    @pl.when((z == 2) | (z == 4))
    def _():
        pair_copy(whole, 1).start()

    @pl.when((z == 1) | (z == 6))
    def _():
        near_copy.start()

    @pl.when(z == 0)
    def _():
        state_out[...] = tree[14, :, WIDTH:]
        state_copy(3).start()
        state_copy(1).start()
        begins[...] = jnp.zeros_like(begins)

    @pl.when(z >= 4)
    def _():
        lax.fori_loop(0, HEADS, inside, 0, unroll=4)

    @pl.when((z == 3) | (z >= 5))
    def _():
        pair_copy(whole, 1).wait_recv()

    @pl.when((z == 3) | (z == 5))
    def _():
        tree[15] = compose(behind[...], tree[14]).astype(BF16)

    @pl.when(z == 5)
    def _():
        pair_copy(tree.at[15], 2).start()
        pair_copy(tree.at[15], 1).start()

    @pl.when((z == 3) | (z == 7))
    def _():
        near_copy.wait_recv()

    @pl.when(z > 0)
    def _():
        state_copy(1).wait_recv()

    @pl.when(z == 1)
    def _():
        state_out[...] = apply(tree[14], state_in[...]).astype(BF16)
        state_copy(1).start()

    @pl.when(z == 3)
    def _():
        begins[...] = apply(near[...], state_in[...]).astype(BF16)
        state_out[...] = apply(tree[15], begins[...]).astype(BF16)
        for ahead in (4, 3, 2, 1):
            state_copy(ahead).start()
        begins[...] = apply(behind[...], begins[...]).astype(BF16)

    @pl.when((z == 1) | (z == 2) | (z == 4))
    def _():
        begins[...] = state_in[...]

    @pl.when(z >= 5)
    def _():
        begins[...] = apply(behind[...], state_in[...]).astype(BF16)

    @pl.when(z == 7)
    def _():
        begins[...] = apply(near[...], begins[...]).astype(BF16)

    begin = {0: begins[...]}
    begin[8] = apply(tree[12], begin[0]).astype(BF16)
    for i in (0, 1):
        begin[8 * i + 4] = apply(tree[8 + 2 * i], begin[8 * i]).astype(BF16)
    for i in range(4):
        begin[4 * i + 2] = apply(tree[2 * i], begin[4 * i]).astype(BF16)
    for i in range(8):
        begin[2 * i + 1] = apply(recv[2 * i], begin[2 * i]).astype(BF16)
    for i in range(HEADS):
        starts[i] = begin[i]

    offsets = OFFSETS[: HEADS - 1]

    def down_copy(step):
        dx, dy = offsets[step]
        px, py = lax.rem(x + dx, SIDE), lax.rem(y + dy, SIDE)
        return pltpu.make_async_remote_copy(
            src_ref=starts.at[px * SIDE + py],
            dst_ref=got.at[mine],
            send_sem=down_send.at[step],
            recv_sem=down_recv.at[mine],
            device_id=in_plane(px, py),
            device_id_type=MESH,
        )

    for step in range(HEADS - 1):
        down_copy(step).start()
    got[mine] = starts[place]

    @pl.when(z < 4)
    def _():
        lax.fori_loop(0, HEADS, inside, 0, unroll=4)

    def await_down(head):
        pltpu.make_async_remote_copy(
            src_ref=starts.at[0],
            dst_ref=got.at[head],
            send_sem=down_send.at[0],
            recv_sem=down_recv.at[head],
            device_id=in_plane(x, y),
            device_id_type=MESH,
        ).wait_recv()

    owners = [mine]
    for dx, dy in offsets:
        owners.append(lax.rem(y + SIDE - dy, SIDE) * SIDE + lax.rem(x + SIDE - dx, SIDE))
    for part in range(SIDE):
        now = owners[SIDE * part : SIDE * part + SIDE]
        for step, head in enumerate(now):
            if part or step:
                await_down(head)
        for head in now:
            attention = inner_out[head] + dot(query_state[head], got[head])
            attention = attention.astype(BF16).astype(F32)
            scale = lax.rsqrt(jnp.mean(attention * attention, -1, keepdims=True) + 1e-05)
            out_ref[:, lanes_of(head)] = (attention * scale * gates[head]).astype(BF16)

    for copy in rims:
        copy.wait_send()

    def settle_up(slot, carry):
        up_copy(slot, x, y).wait_send()
        return carry

    lax.fori_loop(0, HEADS - 1, settle_up, 0)
    for step in range(HEADS - 1):
        down_copy(step).wait_send()

    @pl.when((z == 2) | (z == 4) | (z == 5))
    def _():
        pair_copy(whole, 1).wait_send()

    @pl.when(z == 5)
    def _():
        pair_copy(whole, 2).wait_send()

    @pl.when((z == 1) | (z == 6))
    def _():
        near_copy.wait_send()

    @pl.when((z == 0) | (z == 1) | (z == 3))
    def _():
        state_copy(1).wait_send()

    @pl.when((z == 0) | (z == 3))
    def _():
        state_copy(3).wait_send()

    @pl.when(z == 3)
    def _():
        state_copy(2).wait_send()
        state_copy(4).wait_send()


def layer(depth, query_raw, key_raw, value_raw, log_decay, beta, conv_weight, out_gate, norm_gain):
    rows, width = query_raw.shape
    wide = pltpu.VMEM((rows, width), BF16)
    dma = pltpu.SemaphoreType.DMA
    return pl.pallas_call(
        functools.partial(kernel, depth),
        out_shape=jax.ShapeDtypeStruct((rows, width), BF16),
        in_specs=[pl.BlockSpec(memory_space=pltpu.HBM)] * 8,
        out_specs=pl.BlockSpec(memory_space=pltpu.VMEM),
        scratch_shapes=[wide] * 5
        + [
            pltpu.VMEM(beta.shape[::-1], BF16),
            pltpu.VMEM(conv_weight.shape, F32),
            pltpu.VMEM((1, WIDTH), F32),
            pltpu.VMEM((3, 8, width), BF16),
        ]
        + [wide] * 5
        + [
            pltpu.VMEM((3, 16, width), F32),
            pltpu.VMEM((8, width), F32),
            pltpu.VMEM((HEADS, WIDTH, WIDTH), F32),
            pltpu.VMEM((HEADS, WIDTH, WIDTH), BF16),
            pltpu.VMEM((WIDTH, WIDTH), jnp.int32),
            pltpu.VMEM((HEADS, WIDTH, WIDTH), BF16),
            pltpu.VMEM((HEADS, WIDTH, 2 * WIDTH), BF16),
            pltpu.VMEM((HEADS, WIDTH, WIDTH), F32),
            pltpu.VMEM((HEADS, WIDTH, 2 * WIDTH), BF16),
            pltpu.VMEM((HEADS, WIDTH, 2 * WIDTH), BF16),
            pltpu.VMEM((16, WIDTH, 2 * WIDTH), BF16),
            pltpu.VMEM((WIDTH, 2 * WIDTH), BF16),
            pltpu.VMEM((WIDTH, 2 * WIDTH), BF16),
            pltpu.VMEM((WIDTH, WIDTH), BF16),
            pltpu.VMEM((WIDTH, WIDTH), BF16),
            pltpu.VMEM((WIDTH, WIDTH), BF16),
            pltpu.VMEM((HEADS, WIDTH, WIDTH), BF16),
            pltpu.VMEM((HEADS, WIDTH, WIDTH), BF16),
            dma((8,)),
            dma((3,)),
            dma((3,)),
            dma((HEADS,)),
            dma((HEADS,)),
            dma((2,)),
            dma,
            dma,
            dma,
            dma((4,)),
            dma,
            dma((HEADS,)),
            dma((HEADS,)),
        ],
        compiler_params=pltpu.CompilerParams(
            collective_id=0, has_side_effects=True, vmem_limit_bytes=40 * 2**20
        ),
    )(
        *[
            pltpu.with_memory_space_constraint(array, pltpu.HBM)
            for array in (
                query_raw,
                key_raw,
                value_raw,
                log_decay,
                out_gate,
                beta.T,
                conv_weight,
                norm_gain.reshape(1, WIDTH),
            )
        ]
    )


def solution(mesh):
    tokens = P(("dp", "ctx", "head"), None)
    return jax.shard_map(
        functools.partial(layer, mesh.shape["ctx"] // SIDE),
        mesh=mesh,
        in_specs=(tokens, tokens, tokens, tokens, tokens, P(), tokens, P()),
        out_specs=tokens,
        check_vma=False,
    )
```

```python
import functools

import jax
import jax.numpy as jnp
from jax import lax
from jax.experimental import pallas as pl
from jax.experimental.pallas import tpu as pltpu
from jax.sharding import PartitionSpec as P

MESH = pl.DeviceIdType.MESH
WIDTH = 128
HEADS = 16
SIDE = 4
F32 = jnp.float32
BF16 = jnp.bfloat16


def dot(a, b):
    return jnp.dot(a, b, preferred_element_type=F32)


def dot_nt(a, b):
    return lax.dot_general(a, b, (((1,), (1,)), ((), ())), preferred_element_type=F32)


def dot_tn(a, b):
    return lax.dot_general(a, b, (((0,), (0,)), ((), ())), preferred_element_type=F32)


FAR = 4
OFFSETS = (
    ((1, 1), (3, 3), (2, 0), (0, 2))
    + ((2, 2), (2, 1), (1, 2), (1, 3))
    + ((2, 3), (3, 2), (3, 1), (0, 3))
    + ((1, 0), (3, 0), (0, 1), (0, 0))
)


def entry(position, table):
    if len(table) == 1:
        return table[0]
    half = lax.div(position, 2)
    odd = lax.rem(position, 2) == 1
    return jnp.where(odd, entry(half, table[1::2]), entry(half, table[::2]))


def lanes_of(index):
    return pl.ds(pl.multiple_of(index * WIDTH, WIDTH), WIDTH)


def silu(u):
    return u / (1.0 + jnp.exp(-u))


def compose(first, second):
    return first.astype(F32) - dot(second[:, :WIDTH], first) + second.astype(F32)


def apply(step, state):
    return state.astype(F32) - dot(step[:, :WIDTH], state) + step[:, WIDTH:].astype(F32)


def kernel(
    depth,
    query_hbm,
    key_hbm,
    value_hbm,
    decay_hbm,
    gate_hbm,
    beta_hbm,
    taps_hbm,
    gain_hbm,
    out_ref,
    query_in,
    key_in,
    value_in,
    decay_in,
    gate_in,
    beta_ref,
    taps_ref,
    gain_ref,
    far_beta,
    rim_out,
    rim,
    rise,
    key_mid,
    key_down,
    key_end,
    value_rate,
    edge,
    vectors,
    inner_out,
    query_state,
    level,
    solved_kept,
    gates,
    send,
    recv,
    tree,
    behind,
    near,
    state_in,
    state_out,
    begins,
    starts,
    got,
    load_sem,
    rim_send,
    rim_recv,
    far_send,
    far_recv,
    hint_send,
    hint_recv,
    up_send,
    up_recv,
    pair_send,
    pair_recv,
    near_send,
    near_recv,
    state_send,
    state_recv,
    down_send,
    down_recv,
):
    ctx, y = lax.axis_index("ctx"), lax.axis_index("head")
    x, z = lax.rem(ctx, SIDE), lax.div(ctx, SIDE)
    place = x * SIDE + y
    mine = y * SIDE + x
    total = depth * SIDE * SIDE
    linear = ctx * SIDE + y
    after = lax.rem(linear + 1, total)
    before = lax.rem(linear + total - 1, total)

    def device(cx, cy):
        return {"ctx": cx, "head": cy}

    def in_plane(px, py):
        return device(z * SIDE + px, py)

    def in_line(ahead):
        return device(lax.rem(z + ahead, depth) * SIDE + x, y)

    token_after = device(lax.div(after, SIDE), lax.rem(after, SIDE))
    token_before = device(lax.div(before, SIDE), lax.rem(before, SIDE))

    barrier = pltpu.get_barrier_semaphore()
    for dx in range(SIDE):
        for dy in range(SIDE):
            if dx or dy:
                pl.semaphore_signal(
                    barrier,
                    inc=1,
                    device_id=in_plane(lax.rem(x + dx, SIDE), lax.rem(y + dy, SIDE)),
                    device_id_type=MESH,
                )
    for other in [in_line(ahead) for ahead in range(1, depth)] + [token_after, token_before]:
        pl.semaphore_signal(barrier, inc=1, device_id=other, device_id_type=MESH)

    own = pl.ds(0, HEADS * WIDTH)
    loads = [
        pltpu.make_async_copy(source, target, load_sem.at[i])
        for i, (source, target) in enumerate(
            (
                (decay_hbm, decay_in.at[:, own]),
                (beta_hbm, beta_ref),
                (taps_hbm, taps_ref),
                (key_hbm, key_in.at[:, own]),
                (value_hbm, value_in.at[:, own]),
                (query_hbm, query_in),
                (gate_hbm, gate_in),
                (gain_hbm, gain_ref),
            )
        )
    ]
    for load in loads:
        load.start()

    row = lax.broadcasted_iota(jnp.int32, (WIDTH, WIDTH), 0)
    col = lax.broadcasted_iota(jnp.int32, (WIDTH, WIDTH), 1)
    apart = jnp.bitwise_xor(row, col)
    depth_of = jnp.where(row >= col, 0, -1)
    for bit in range(7):
        depth_of = depth_of + jnp.where((row > col) & (apart >= 2**bit), 1, 0)
    level[...] = depth_of

    for load in loads[:5]:
        load.wait()
    tail = pl.ds(WIDTH - 8, 8)
    late = lax.broadcasted_iota(jnp.int32, rim_out.shape, 0) >= 5
    rim_out[...] = jnp.where(
        late, key_in[tail, own].astype(F32), pltpu.roll(value_in[tail, own].astype(F32), 5, 0)
    ).astype(BF16)

    pl.semaphore_wait(barrier, SIDE * SIDE - 1 + depth - 1 + 2)

    rims = [
        pltpu.make_async_remote_copy(
            src_ref=source,
            dst_ref=rim.at[i, :, own],
            send_sem=rim_send.at[i],
            recv_sem=rim_recv.at[i],
            device_id=token_after,
            device_id_type=MESH,
        )
        for i, source in enumerate((rim_out, query_hbm.at[tail, :]))
    ]
    for copy in rims:
        copy.start()

    def far_copy(source, target, sent, landed, px, py):
        return pltpu.make_async_remote_copy(
            src_ref=source,
            dst_ref=target,
            send_sem=sent,
            recv_sem=landed,
            device_id=in_plane(px, py),
            device_id_type=MESH,
        )

    fars, hints, sources = [], [], []
    for i, (dx, dy) in enumerate(OFFSETS[:FAR]):
        px, py = lax.rem(x + dx, SIDE), lax.rem(y + dy, SIDE)
        sources.append((lax.rem(x + SIDE - dx, SIDE), lax.rem(y + SIDE - dy, SIDE)))
        here, there = lanes_of(py * SIDE + px), pl.ds((HEADS + i) * WIDTH, WIDTH)
        pairs = [(array.at[:, here], array.at[:, there]) for array in (key_in, value_in, decay_in)]
        for j, (source, target) in enumerate(pairs + [(beta_ref, far_beta.at[i])]):
            fars.append(
                far_copy(
                    source, target, far_send.at[FAR * i + j], far_recv.at[FAR * i + j], px, py
                )
            )
        hints.append(
            far_copy(
                rim.at[0, :, here], rim.at[0, :, there], hint_send.at[i], hint_recv.at[i], px, py
            )
        )
    def weigh(values, lanes, which):
        total_sum = taps_ref[which, 3:4, lanes] * values
        for back in range(1, 4):
            total_sum += taps_ref[which, 3 - back : 4 - back, lanes] * pltpu.roll(values, back, 0)
        return total_sum

    def rounded(sums):
        return silu(sums).astype(BF16).astype(F32)

    def lay_down(count, lanes, key_sum, value_sum, up, down, rate, end_row):
        rows = pl.ds(0, count)
        keys, values = rounded(key_sum), rounded(value_sum)
        keys = keys * lax.rsqrt(jnp.sum(keys * keys, -1, keepdims=True) + 1e-06)
        falling = keys * down
        key_mid[rows, lanes] = (rate * keys * up).astype(BF16)
        key_down[rows, lanes] = falling.astype(BF16)
        key_end[rows, lanes] = (falling * end_row).astype(BF16)
        value_rate[rows, lanes] = (rate * values).astype(BF16)

    def past_rows(index, lanes, begun, turn=0):
        past = jnp.where(begun, rim[index, :, lanes].astype(F32), 0.0)
        return pltpu.roll(past, turn, 0) if turn else past

    def prepare(lanes, taps, rates, head):
        lower = jnp.where(level[...] >= 0, 1.0, 0.0).astype(BF16)
        cumul = dot(lower, decay_in[:, lanes])
        middle = cumul[WIDTH // 2 - 1 : WIDTH // 2]
        last = cumul[WIDTH - 1 : WIDTH]
        up, down = jnp.exp(cumul - middle), jnp.exp(middle - cumul)
        end_row = jnp.exp(last - middle)
        chosen = lax.broadcasted_iota(jnp.int32, (HEADS, WIDTH), 0) == head
        rate = dot_tn(rates, jnp.where(chosen, 1.0, 0.0).astype(BF16))
        vectors[0:1, lanes] = jnp.exp(middle)
        vectors[1:2, lanes] = jnp.exp(last)
        vectors[2:3, lanes] = end_row
        rise[:, lanes] = up
        edge[0, :, lanes] = down[:16]
        edge[1, :, lanes] = rate[:16]
        key_sum = weigh(key_in[:, lanes].astype(F32), taps, 1)
        value_sum = weigh(value_in[:, lanes].astype(F32), taps, 2)
        lay_down(WIDTH, lanes, key_sum, value_sum, up, down, rate, end_row)

    def prepare_own(head, carry):
        prepare(lanes_of(head), lanes_of(head), beta_ref[...], head)
        return carry

    def prepare_far(i, carry):
        prepare(lanes_of(HEADS + i), lanes_of(mine), far_beta[i], mine)
        return carry

    lax.fori_loop(0, HEADS, prepare_own, 0, unroll=2)

    for copy in fars:
        copy.start()

    rims[0].wait_recv()
    for copy in hints:
        copy.start()

    def spot_at(position):
        dx, dy = [entry(position, [offset[axis] for offset in OFFSETS]) for axis in (0, 1)]
        return lax.rem(x + dx, SIDE), lax.rem(y + dy, SIDE)

    def mend(lanes, taps, begun):
        sums = []
        for which, source, turn in ((1, key_in, 0), (2, value_in, 3)):
            both = [past_rows(0, lanes, begun, turn), source[0:16, lanes].astype(F32)]
            sums.append(weigh(jnp.concatenate(both, 0), taps, which)[8:])
        lay_down(
            16,
            lanes,
            *sums,
            rise[0:16, lanes],
            edge[0, :, lanes],
            edge[1, :, lanes],
            vectors[2:3, lanes],
        )

    def up_copy(slot, px, py):
        return pltpu.make_async_remote_copy(
            src_ref=send.at[slot],
            dst_ref=recv.at[place],
            send_sem=up_send.at[slot],
            recv_sem=up_recv.at[place],
            device_id=in_plane(px, py),
            device_id_type=MESH,
        )

    def solve(lanes, taps, begun):
        many = range(len(lanes))
        for i in many:
            mend(lanes[i], taps[i], begun[i])
        depths = level[...]
        zero = jnp.zeros((WIDTH, WIDTH), BF16)
        one = jnp.where(depths == 0, 1.0, 0.0).astype(BF16)
        lower, rest, inverse, right, solved = [], [], [], [], []
        for i in many:
            exact = jnp.where(depths > 0, dot_nt(key_mid[:, lanes[i]], key_down[:, lanes[i]]), 0.0)
            lower.append(exact.astype(BF16))
            rest.append((exact - lower[i].astype(F32)).astype(BF16))
            inverse.append(one - jnp.where(depths == 1, lower[i], zero))
            right.append(jnp.concatenate([value_rate[:, lanes[i]], key_mid[:, lanes[i]]], 1))
        guess = []
        for step in (2, 4, 6):
            near_part = (depths == step) | (depths == step + 1)
            fall = [jnp.where(near_part, lower[i], zero) for i in many]
            if step == 6:
                fall = [jnp.concatenate([fall[i], right[i]], 1) for i in many]
            parts = [dot(inverse[i], fall[i]) for i in many]
            bases = [inverse[i].astype(F32) for i in many]
            if step == 6:
                bases = [jnp.concatenate([bases[i], parts[i][:, WIDTH:]], 1) for i in many]
            parts = [parts[i][:, :WIDTH].astype(BF16) for i in many]
            twice = [
                dot(parts[i], jnp.concatenate([parts[i], bases[i].astype(BF16)], 1)) for i in many
            ]
            halves = [bases[i] - twice[i][:, WIDTH:] for i in many]
            halves = [
                halves[i] + dot(twice[i][:, :WIDTH].astype(BF16), halves[i].astype(BF16))
                for i in many
            ]
            inverse = [halves[i][:, :WIDTH].astype(BF16) for i in many]
            if step == 6:
                guess = [halves[i][:, WIDTH:].astype(BF16) for i in many]
        miss = [
            right[i].astype(F32)
            - guess[i].astype(F32)
            - dot(
                jnp.concatenate([lower[i], rest[i]], 1), jnp.concatenate([guess[i], guess[i]], 0)
            )
            for i in many
        ]
        solved = [
            (guess[i].astype(F32) + dot(inverse[i], miss[i].astype(BF16))).astype(BF16)
            for i in many
        ]
        return solved

    def pack(lanes, solution_rows):
        ends = dot_tn(key_end[:, lanes], solution_rows)
        diagonal = jnp.where(level[...] == 0, 1.0 - vectors[1:2, lanes], 0.0)
        left = ends[:, WIDTH:] * vectors[0:1, lanes] + diagonal
        return jnp.concatenate([left, ends[:, :WIDTH]], 1).astype(BF16)

    def solve_own(heads):
        lanes = [lanes_of(head) for head in heads]
        solved = solve(lanes, lanes, [linear > 0] * len(heads))
        for head, solution_rows in zip(heads, solved):
            solved_kept[head] = solution_rows
        return [(lanes[i], solved[i]) for i in range(len(heads))]

    def turns(turn, carry):
        positions = [SIDE * turn + i for i in range(SIDE)]
        spots = [spot_at(position) for position in positions]
        packs = [pack(*pair) for pair in solve_own([py * SIDE + px for px, py in spots])]
        for i in range(SIDE):

            def leave(i=i):
                send[positions[i]] = packs[i]
                up_copy(positions[i], *spots[i]).start()

            def keep(i=i):
                recv[place] = packs[i]

            if i == SIDE - 1:
                pl.when(turn < SIDE - 1)(leave)
                pl.when(turn == SIDE - 1)(keep)
            else:
                leave()
        return carry

    lax.fori_loop(1, SIDE, turns, 0)

    for copy in fars + hints:
        copy.wait_recv()
    lax.fori_loop(0, FAR, prepare_far, 0, unroll=2)
    far_lanes = [lanes_of(HEADS + i) for i in range(FAR)]
    far_begun = [z + px + py > 0 for px, py in sources]
    far_solved = solve(far_lanes, [lanes_of(mine)] * FAR, far_begun)
    for i, (px, py) in enumerate(sources):
        recv[px * SIDE + py] = pack(far_lanes[i], far_solved[i])

    def await_up(source, carry):
        local = source == place
        for px, py in sources:
            local = local | (source == px * SIDE + py)

        @pl.when(jnp.logical_not(local))
        def _():
            pltpu.make_async_remote_copy(
                src_ref=send.at[0],
                dst_ref=recv.at[source],
                send_sem=up_send.at[0],
                recv_sem=up_recv.at[source],
                device_id=in_plane(x, y),
                device_id_type=MESH,
            ).wait_recv()

        return carry

    lax.fori_loop(0, HEADS, await_up, 0)

    for i in range(8):
        tree[i] = compose(recv[2 * i], recv[2 * i + 1]).astype(BF16)
    for i in range(4):
        tree[8 + i] = compose(tree[2 * i], tree[2 * i + 1]).astype(BF16)
    for i in range(2):
        tree[12 + i] = compose(tree[8 + 2 * i], tree[9 + 2 * i]).astype(BF16)
    tree[14] = compose(tree[12], tree[13]).astype(BF16)

    def inside(head, carry):
        lanes = lanes_of(head)
        both = jnp.concatenate([past_rows(1, lanes, linear > 0), query_in[:, lanes].astype(F32)], 0)
        query = (rounded(weigh(both, lanes, 0)[8:]) * rise[:, lanes]).astype(BF16)
        scores = jnp.where(level[...] >= 0, dot_nt(query, key_down[:, lanes]), 0.0).astype(BF16)
        inner = dot(scores, solved_kept[head])
        inner_out[head] = inner[:, :WIDTH]
        query_state[head] = (
            (query.astype(F32) - inner[:, WIDTH:]) * vectors[0:1, lanes]
        ).astype(BF16)
        gate = 1.0 / (1.0 + jnp.exp(-gate_in[:, lanes].astype(F32)))
        gates[head] = gain_ref[...] * gate
        return carry

    def finish_inside():
        spots = [(lax.rem(x + dx, SIDE), lax.rem(y + dy, SIDE)) for dx, dy in OFFSETS[:FAR]]
        solve_own([py * SIDE + px for px, py in spots])
        lax.fori_loop(0, HEADS, inside, 0, unroll=4)

    for load in loads[5:]:
        load.wait()
    rims[1].wait_recv()

    def z_copy(source, target, sent, landed, ahead):
        return pltpu.make_async_remote_copy(
            src_ref=source,
            dst_ref=target,
            send_sem=sent,
            recv_sem=landed,
            device_id=in_line(ahead),
            device_id_type=MESH,
        )

    def pair_copy(source, ahead):
        return z_copy(source, behind, pair_send.at[ahead - 1], pair_recv, ahead)

    def state_copy(ahead):
        return z_copy(state_out, state_in, state_send.at[ahead - 1], state_recv, ahead)

    whole = tree.at[14]
    near_copy = z_copy(whole, near, near_send, near_recv, jnp.where(z == 1, 2, 1))

    @pl.when((z == 2) | (z == 4))
    def _():
        pair_copy(whole, 1).start()

    @pl.when((z == 1) | (z == 6))
    def _():
        near_copy.start()

    @pl.when(z == 0)
    def _():
        state_out[...] = tree[14, :, WIDTH:]
        state_copy(3).start()
        state_copy(1).start()
        begins[...] = jnp.zeros_like(begins)

    @pl.when((z == 3) | (z == 5))
    def _():
        pair_copy(whole, 1).wait_recv()
        tree[15] = compose(behind[...], tree[14]).astype(BF16)

    @pl.when(z == 5)
    def _():
        pair_copy(tree.at[15], 2).start()
        pair_copy(tree.at[15], 1).start()

    @pl.when(z >= 4)
    def _():
        finish_inside()

    @pl.when(z >= 6)
    def _():
        pair_copy(whole, 1).wait_recv()

    @pl.when((z == 3) | (z == 7))
    def _():
        near_copy.wait_recv()

    @pl.when(z > 0)
    def _():
        state_copy(1).wait_recv()

    @pl.when(z == 1)
    def _():
        state_out[...] = apply(tree[14], state_in[...]).astype(BF16)
        state_copy(1).start()

    @pl.when(z == 3)
    def _():
        begins[...] = apply(near[...], state_in[...]).astype(BF16)
        state_out[...] = apply(tree[15], begins[...]).astype(BF16)
        for ahead in (4, 3, 2, 1):
            state_copy(ahead).start()
        begins[...] = apply(behind[...], begins[...]).astype(BF16)

    @pl.when((z == 1) | (z == 2) | (z == 4))
    def _():
        begins[...] = state_in[...]

    @pl.when(z >= 5)
    def _():
        begins[...] = apply(behind[...], state_in[...]).astype(BF16)

    @pl.when(z == 7)
    def _():
        begins[...] = apply(near[...], begins[...]).astype(BF16)

    begin = {0: begins[...]}
    begin[8] = apply(tree[12], begin[0]).astype(BF16)
    for i in (0, 1):
        begin[8 * i + 4] = apply(tree[8 + 2 * i], begin[8 * i]).astype(BF16)
    for i in range(4):
        begin[4 * i + 2] = apply(tree[2 * i], begin[4 * i]).astype(BF16)
    for i in range(8):
        begin[2 * i + 1] = apply(recv[2 * i], begin[2 * i]).astype(BF16)
    for i in range(HEADS):
        starts[i] = begin[i]

    offsets = sorted(
        OFFSETS[: HEADS - 1], key=lambda offset: -sum(min(d, SIDE - d) for d in offset)
    )

    def down_copy(step):
        dx, dy = offsets[step]
        px, py = lax.rem(x + dx, SIDE), lax.rem(y + dy, SIDE)
        return pltpu.make_async_remote_copy(
            src_ref=starts.at[px * SIDE + py],
            dst_ref=got.at[mine],
            send_sem=down_send.at[step],
            recv_sem=down_recv.at[mine],
            device_id=in_plane(px, py),
            device_id_type=MESH,
        )

    for step in range(HEADS - 1):
        down_copy(step).start()
    got[mine] = starts[place]

    @pl.when(z < 4)
    def _():
        finish_inside()

    def await_down(head):
        pltpu.make_async_remote_copy(
            src_ref=starts.at[0],
            dst_ref=got.at[head],
            send_sem=down_send.at[0],
            recv_sem=down_recv.at[head],
            device_id=in_plane(x, y),
            device_id_type=MESH,
        ).wait_recv()

    owners = [mine]
    for dx, dy in offsets:
        owners.append(lax.rem(y + SIDE - dy, SIDE) * SIDE + lax.rem(x + SIDE - dx, SIDE))
    for part in range(SIDE):
        now = owners[SIDE * part : SIDE * part + SIDE]
        for step, head in enumerate(now):
            if part or step:
                await_down(head)
        for head in now:
            attention = inner_out[head] + dot(query_state[head], got[head])
            attention = attention.astype(BF16).astype(F32)
            scale = lax.rsqrt(jnp.mean(attention * attention, -1, keepdims=True) + 1e-05)
            out_ref[:, lanes_of(head)] = (attention * scale * gates[head]).astype(BF16)

    for copy in rims:
        copy.wait_send()

    def settle_up(slot, carry):
        up_copy(slot, x, y).wait_send()
        return carry

    lax.fori_loop(FAR, HEADS - 1, settle_up, 0)
    for copy in fars + hints:
        copy.wait_send()
    for step in range(HEADS - 1):
        down_copy(step).wait_send()

    @pl.when((z == 2) | (z == 4) | (z == 5))
    def _():
        pair_copy(whole, 1).wait_send()

    @pl.when(z == 5)
    def _():
        pair_copy(whole, 2).wait_send()

    @pl.when((z == 1) | (z == 6))
    def _():
        near_copy.wait_send()

    @pl.when((z == 0) | (z == 1) | (z == 3))
    def _():
        state_copy(1).wait_send()

    @pl.when((z == 0) | (z == 3))
    def _():
        state_copy(3).wait_send()

    @pl.when(z == 3)
    def _():
        state_copy(2).wait_send()
        state_copy(4).wait_send()


def layer(depth, query_raw, key_raw, value_raw, log_decay, beta, conv_weight, out_gate, norm_gain):
    rows, width = query_raw.shape
    wide = pltpu.VMEM((rows, width), BF16)
    more = width + FAR * WIDTH
    wider = pltpu.VMEM((rows, more), BF16)
    dma = pltpu.SemaphoreType.DMA
    return pl.pallas_call(
        functools.partial(kernel, depth),
        out_shape=jax.ShapeDtypeStruct((rows, width), BF16),
        in_specs=[pl.BlockSpec(memory_space=pltpu.HBM)] * 8,
        out_specs=pl.BlockSpec(memory_space=pltpu.VMEM),
        scratch_shapes=[wide, wider, wider, wider, wide]
        + [
            pltpu.VMEM(beta.shape[::-1], BF16),
            pltpu.VMEM(conv_weight.shape, F32),
            pltpu.VMEM((1, WIDTH), F32),
            pltpu.VMEM((FAR, HEADS, WIDTH), BF16),
            pltpu.VMEM((8, width), BF16),
            pltpu.VMEM((2, 8, more), BF16),
            pltpu.VMEM((rows, more), F32),
        ]
        + [wider] * 4
        + [
            pltpu.VMEM((2, 16, more), F32),
            pltpu.VMEM((8, more), F32),
            pltpu.VMEM((HEADS, WIDTH, WIDTH), F32),
            pltpu.VMEM((HEADS, WIDTH, WIDTH), BF16),
            pltpu.VMEM((WIDTH, WIDTH), jnp.int32),
            pltpu.VMEM((HEADS, WIDTH, 2 * WIDTH), BF16),
            pltpu.VMEM((HEADS, WIDTH, WIDTH), F32),
            pltpu.VMEM((HEADS, WIDTH, 2 * WIDTH), BF16),
            pltpu.VMEM((HEADS, WIDTH, 2 * WIDTH), BF16),
            pltpu.VMEM((16, WIDTH, 2 * WIDTH), BF16),
            pltpu.VMEM((WIDTH, 2 * WIDTH), BF16),
            pltpu.VMEM((WIDTH, 2 * WIDTH), BF16),
            pltpu.VMEM((WIDTH, WIDTH), BF16),
            pltpu.VMEM((WIDTH, WIDTH), BF16),
            pltpu.VMEM((WIDTH, WIDTH), BF16),
            pltpu.VMEM((HEADS, WIDTH, WIDTH), BF16),
            pltpu.VMEM((HEADS, WIDTH, WIDTH), BF16),
            dma((8,)),
            dma((2,)),
            dma((2,)),
            dma((FAR * FAR,)),
            dma((FAR * FAR,)),
            dma((FAR,)),
            dma((FAR,)),
            dma((HEADS,)),
            dma((HEADS,)),
            dma((2,)),
            dma,
            dma,
            dma,
            dma((4,)),
            dma,
            dma((HEADS,)),
            dma((HEADS,)),
        ],
        compiler_params=pltpu.CompilerParams(
            collective_id=0, has_side_effects=True, vmem_limit_bytes=40 * 2**20
        ),
    )(
        *[
            pltpu.with_memory_space_constraint(array, pltpu.HBM)
            for array in (
                query_raw,
                key_raw,
                value_raw,
                log_decay,
                out_gate,
                beta.T,
                conv_weight,
                norm_gain.reshape(1, WIDTH),
            )
        ]
    )


def solution(mesh):
    tokens = P(("dp", "ctx", "head"), None)
    return jax.shard_map(
        functools.partial(layer, mesh.shape["ctx"] // SIDE),
        mesh=mesh,
        in_specs=(tokens, tokens, tokens, tokens, tokens, P(), tokens, P()),
        out_specs=tokens,
        check_vma=False,
    )
```

```python
import functools

import jax
import jax.numpy as jnp
from jax import lax
from jax.experimental import pallas as pl
from jax.experimental.pallas import tpu as pltpu
from jax.sharding import PartitionSpec as P

MESH = pl.DeviceIdType.MESH
WIDTH = 128
HEADS = 16
SIDE = 4
F32 = jnp.float32
BF16 = jnp.bfloat16


def dot(a, b):
    return jnp.dot(a, b, preferred_element_type=F32)


def dot_nt(a, b):
    return lax.dot_general(a, b, (((1,), (1,)), ((), ())), preferred_element_type=F32)


def dot_tn(a, b):
    return lax.dot_general(a, b, (((0,), (0,)), ((), ())), preferred_element_type=F32)


FAR = 4
OFFSETS = (
    ((1, 1), (3, 3), (2, 0), (0, 2))
    + ((2, 2), (2, 1), (1, 2), (1, 3))
    + ((2, 3), (3, 2), (3, 1), (0, 3))
    + ((1, 0), (3, 0), (0, 1), (0, 0))
)


def entry(position, table):
    if len(table) == 1:
        return table[0]
    half = lax.div(position, 2)
    odd = lax.rem(position, 2) == 1
    return jnp.where(odd, entry(half, table[1::2]), entry(half, table[::2]))


def lanes_of(index):
    return pl.ds(pl.multiple_of(index * WIDTH, WIDTH), WIDTH)


def silu(u):
    return u / (1.0 + jnp.exp(-u))


def compose(first, second):
    return first.astype(F32) - dot(second[:, :WIDTH], first) + second.astype(F32)


def apply(step, state):
    return state.astype(F32) - dot(step[:, :WIDTH], state) + step[:, WIDTH:].astype(F32)


def kernel(
    depth,
    query_hbm,
    key_hbm,
    value_hbm,
    decay_hbm,
    gate_hbm,
    beta_hbm,
    taps_hbm,
    gain_hbm,
    out_ref,
    query_in,
    key_in,
    value_in,
    decay_in,
    gate_in,
    beta_ref,
    taps_ref,
    gain_ref,
    far_beta,
    rim_out,
    rim,
    rise,
    key_mid,
    key_down,
    key_end,
    value_rate,
    edge,
    vectors,
    inner_out,
    query_state,
    level,
    solved_kept,
    gates,
    send,
    recv,
    tree,
    behind,
    near,
    state_in,
    state_out,
    begins,
    starts,
    got,
    load_sem,
    rim_send,
    rim_recv,
    far_send,
    far_recv,
    hint_send,
    hint_recv,
    up_send,
    up_recv,
    pair_send,
    pair_recv,
    near_send,
    near_recv,
    state_send,
    state_recv,
    down_send,
    down_recv,
):
    ctx, y = lax.axis_index("ctx"), lax.axis_index("head")
    x, z = lax.rem(ctx, SIDE), lax.div(ctx, SIDE)
    place = x * SIDE + y
    mine = y * SIDE + x
    total = depth * SIDE * SIDE
    linear = ctx * SIDE + y
    after = lax.rem(linear + 1, total)
    before = lax.rem(linear + total - 1, total)

    def device(cx, cy):
        return {"ctx": cx, "head": cy}

    def in_plane(px, py):
        return device(z * SIDE + px, py)

    def in_line(ahead):
        return device(lax.rem(z + ahead, depth) * SIDE + x, y)

    token_after = device(lax.div(after, SIDE), lax.rem(after, SIDE))
    token_before = device(lax.div(before, SIDE), lax.rem(before, SIDE))

    barrier = pltpu.get_barrier_semaphore()
    for dx in range(SIDE):
        for dy in range(SIDE):
            if dx or dy:
                pl.semaphore_signal(
                    barrier,
                    inc=1,
                    device_id=in_plane(lax.rem(x + dx, SIDE), lax.rem(y + dy, SIDE)),
                    device_id_type=MESH,
                )
    for other in [in_line(ahead) for ahead in range(1, depth)] + [token_after, token_before]:
        pl.semaphore_signal(barrier, inc=1, device_id=other, device_id_type=MESH)

    own = pl.ds(0, HEADS * WIDTH)
    loads = [
        pltpu.make_async_copy(source, target, load_sem.at[i])
        for i, (source, target) in enumerate(
            (
                (decay_hbm, decay_in.at[:, own]),
                (beta_hbm, beta_ref),
                (taps_hbm, taps_ref),
                (key_hbm, key_in.at[:, own]),
                (value_hbm, value_in.at[:, own]),
                (query_hbm, query_in),
                (gate_hbm, gate_in),
                (gain_hbm, gain_ref),
            )
        )
    ]
    for load in loads:
        load.start()

    row = lax.broadcasted_iota(jnp.int32, (WIDTH, WIDTH), 0)
    col = lax.broadcasted_iota(jnp.int32, (WIDTH, WIDTH), 1)
    apart = jnp.bitwise_xor(row, col)
    depth_of = jnp.where(row >= col, 0, -1)
    for bit in range(7):
        depth_of = depth_of + jnp.where((row > col) & (apart >= 2**bit), 1, 0)
    level[...] = depth_of

    for load in loads[:5]:
        load.wait()
    tail = pl.ds(WIDTH - 8, 8)
    late = lax.broadcasted_iota(jnp.int32, rim_out.shape, 0) >= 5
    rim_out[...] = jnp.where(
        late, key_in[tail, own].astype(F32), pltpu.roll(value_in[tail, own].astype(F32), 5, 0)
    ).astype(BF16)

    pl.semaphore_wait(barrier, SIDE * SIDE - 1 + depth - 1 + 2)

    rims = [
        pltpu.make_async_remote_copy(
            src_ref=source,
            dst_ref=rim.at[i, :, own],
            send_sem=rim_send.at[i],
            recv_sem=rim_recv.at[i],
            device_id=token_after,
            device_id_type=MESH,
        )
        for i, source in enumerate((rim_out, query_hbm.at[tail, :]))
    ]
    for copy in rims:
        copy.start()

    def far_copy(source, target, sent, landed, px, py):
        return pltpu.make_async_remote_copy(
            src_ref=source,
            dst_ref=target,
            send_sem=sent,
            recv_sem=landed,
            device_id=in_plane(px, py),
            device_id_type=MESH,
        )

    fars, hints, sources = [], [], []
    for i, (dx, dy) in enumerate(OFFSETS[:FAR]):
        px, py = lax.rem(x + dx, SIDE), lax.rem(y + dy, SIDE)
        sources.append((lax.rem(x + SIDE - dx, SIDE), lax.rem(y + SIDE - dy, SIDE)))
        here, there = lanes_of(py * SIDE + px), pl.ds((HEADS + i) * WIDTH, WIDTH)
        pairs = [(array.at[:, here], array.at[:, there]) for array in (key_in, value_in, decay_in)]
        for j, (source, target) in enumerate(pairs + [(beta_ref, far_beta.at[i])]):
            fars.append(
                far_copy(
                    source, target, far_send.at[FAR * i + j], far_recv.at[FAR * i + j], px, py
                )
            )
        hints.append(
            far_copy(
                rim.at[0, :, here], rim.at[0, :, there], hint_send.at[i], hint_recv.at[i], px, py
            )
        )
    def weigh(values, lanes, which):
        total_sum = taps_ref[which, 3:4, lanes] * values
        for back in range(1, 4):
            total_sum += taps_ref[which, 3 - back : 4 - back, lanes] * pltpu.roll(values, back, 0)
        return total_sum

    def rounded(sums):
        return silu(sums).astype(BF16).astype(F32)

    def lay_down(count, lanes, key_sum, value_sum, up, down, rate, end_row):
        rows = pl.ds(0, count)
        keys, values = rounded(key_sum), rounded(value_sum)
        keys = keys * lax.rsqrt(jnp.sum(keys * keys, -1, keepdims=True) + 1e-06)
        falling = keys * down
        key_mid[rows, lanes] = (rate * keys * up).astype(BF16)
        key_down[rows, lanes] = falling.astype(BF16)
        key_end[rows, lanes] = (falling * end_row).astype(BF16)
        value_rate[rows, lanes] = (rate * values).astype(BF16)

    def past_rows(index, lanes, begun, turn=0):
        past = jnp.where(begun, rim[index, :, lanes].astype(F32), 0.0)
        return pltpu.roll(past, turn, 0) if turn else past

    def prepare(lanes, taps, rates, head):
        lower = jnp.where(level[...] >= 0, 1.0, 0.0).astype(BF16)
        cumul = dot(lower, decay_in[:, lanes])
        middle = cumul[WIDTH // 2 - 1 : WIDTH // 2]
        last = cumul[WIDTH - 1 : WIDTH]
        up, down = jnp.exp(cumul - middle), jnp.exp(middle - cumul)
        end_row = jnp.exp(last - middle)
        chosen = lax.broadcasted_iota(jnp.int32, (HEADS, WIDTH), 0) == head
        rate = dot_tn(rates, jnp.where(chosen, 1.0, 0.0).astype(BF16))
        vectors[0:1, lanes] = jnp.exp(middle)
        vectors[1:2, lanes] = jnp.exp(last)
        vectors[2:3, lanes] = end_row
        rise[:, lanes] = up
        edge[0, :, lanes] = down[:16]
        edge[1, :, lanes] = rate[:16]
        key_sum = weigh(key_in[:, lanes].astype(F32), taps, 1)
        value_sum = weigh(value_in[:, lanes].astype(F32), taps, 2)
        lay_down(WIDTH, lanes, key_sum, value_sum, up, down, rate, end_row)

    def prepare_own(head, carry):
        prepare(lanes_of(head), lanes_of(head), beta_ref[...], head)
        return carry

    def prepare_far(i, carry):
        prepare(lanes_of(HEADS + i), lanes_of(mine), far_beta[i], mine)
        return carry

    lax.fori_loop(0, 8, prepare_own, 0, unroll=2)
    for copy in fars:
        copy.start()

    lax.fori_loop(8, HEADS, prepare_own, 0, unroll=2)

    rims[0].wait_recv()
    for copy in hints:
        copy.start()

    def spot_at(position):
        dx, dy = [entry(position, [offset[axis] for offset in OFFSETS]) for axis in (0, 1)]
        return lax.rem(x + dx, SIDE), lax.rem(y + dy, SIDE)

    def mend(lanes, taps, begun):
        sums = []
        for which, source, turn in ((1, key_in, 0), (2, value_in, 3)):
            both = [past_rows(0, lanes, begun, turn), source[0:16, lanes].astype(F32)]
            sums.append(weigh(jnp.concatenate(both, 0), taps, which)[8:])
        lay_down(
            16,
            lanes,
            *sums,
            rise[0:16, lanes],
            edge[0, :, lanes],
            edge[1, :, lanes],
            vectors[2:3, lanes],
        )

    def up_copy(slot, px, py):
        return pltpu.make_async_remote_copy(
            src_ref=send.at[slot],
            dst_ref=recv.at[place],
            send_sem=up_send.at[slot],
            recv_sem=up_recv.at[place],
            device_id=in_plane(px, py),
            device_id_type=MESH,
        )

    def solve(lanes, taps, begun):
        many = range(len(lanes))
        for i in many:
            mend(lanes[i], taps[i], begun[i])
        depths = level[...]
        zero = jnp.zeros((WIDTH, WIDTH), BF16)
        one = jnp.where(depths == 0, 1.0, 0.0).astype(BF16)
        lower, rest, inverse, right, solved = [], [], [], [], []
        for i in many:
            exact = jnp.where(depths > 0, dot_nt(key_mid[:, lanes[i]], key_down[:, lanes[i]]), 0.0)
            lower.append(exact.astype(BF16))
            rest.append((exact - lower[i].astype(F32)).astype(BF16))
            inverse.append(one - jnp.where(depths == 1, lower[i], zero))
            right.append(jnp.concatenate([value_rate[:, lanes[i]], key_mid[:, lanes[i]]], 1))
        guess = []
        for step in (2, 4, 6):
            near_part = (depths == step) | (depths == step + 1)
            fall = [jnp.where(near_part, lower[i], zero) for i in many]
            if step == 6:
                fall = [jnp.concatenate([fall[i], right[i]], 1) for i in many]
            parts = [dot(inverse[i], fall[i]) for i in many]
            bases = [inverse[i].astype(F32) for i in many]
            if step == 6:
                bases = [jnp.concatenate([bases[i], parts[i][:, WIDTH:]], 1) for i in many]
            parts = [parts[i][:, :WIDTH].astype(BF16) for i in many]
            twice = [
                dot(parts[i], jnp.concatenate([parts[i], bases[i].astype(BF16)], 1)) for i in many
            ]
            halves = [bases[i] - twice[i][:, WIDTH:] for i in many]
            halves = [
                halves[i] + dot(twice[i][:, :WIDTH].astype(BF16), halves[i].astype(BF16))
                for i in many
            ]
            inverse = [halves[i][:, :WIDTH].astype(BF16) for i in many]
            if step == 6:
                guess = [halves[i][:, WIDTH:].astype(BF16) for i in many]
        miss = [
            right[i].astype(F32)
            - guess[i].astype(F32)
            - dot(
                jnp.concatenate([lower[i], rest[i]], 1), jnp.concatenate([guess[i], guess[i]], 0)
            )
            for i in many
        ]
        solved = [
            (guess[i].astype(F32) + dot(inverse[i], miss[i].astype(BF16))).astype(BF16)
            for i in many
        ]
        return solved

    def pack(lanes, solution_rows):
        ends = dot_tn(key_end[:, lanes], solution_rows)
        diagonal = jnp.where(level[...] == 0, 1.0 - vectors[1:2, lanes], 0.0)
        left = ends[:, WIDTH:] * vectors[0:1, lanes] + diagonal
        return jnp.concatenate([left, ends[:, :WIDTH]], 1).astype(BF16)

    def solve_own(heads):
        lanes = [lanes_of(head) for head in heads]
        solved = solve(lanes, lanes, [linear > 0] * len(heads))
        for head, solution_rows in zip(heads, solved):
            solved_kept[head] = solution_rows
        return [(lanes[i], solved[i]) for i in range(len(heads))]

    def turns(turn, carry):
        positions = [SIDE * turn + i for i in range(SIDE)]
        spots = [spot_at(position) for position in positions]
        packs = [pack(*pair) for pair in solve_own([py * SIDE + px for px, py in spots])]
        for i in range(SIDE):

            def leave(i=i):
                send[positions[i]] = packs[i]
                up_copy(positions[i], *spots[i]).start()

            def keep(i=i):
                recv[place] = packs[i]

            if i == SIDE - 1:
                pl.when(turn < SIDE - 1)(leave)
                pl.when(turn == SIDE - 1)(keep)
            else:
                leave()
        return carry

    lax.fori_loop(1, SIDE, turns, 0)

    for copy in fars + hints:
        copy.wait_recv()
    lax.fori_loop(0, FAR, prepare_far, 0, unroll=2)
    far_lanes = [lanes_of(HEADS + i) for i in range(FAR)]
    far_begun = [z + px + py > 0 for px, py in sources]
    far_solved = solve(far_lanes, [lanes_of(mine)] * FAR, far_begun)
    for i, (px, py) in enumerate(sources):
        recv[px * SIDE + py] = pack(far_lanes[i], far_solved[i])

    def await_up(source, carry):
        local = source == place
        for px, py in sources:
            local = local | (source == px * SIDE + py)

        @pl.when(jnp.logical_not(local))
        def _():
            pltpu.make_async_remote_copy(
                src_ref=send.at[0],
                dst_ref=recv.at[source],
                send_sem=up_send.at[0],
                recv_sem=up_recv.at[source],
                device_id=in_plane(x, y),
                device_id_type=MESH,
            ).wait_recv()

        return carry

    lax.fori_loop(0, HEADS, await_up, 0)

    for i in range(8):
        tree[i] = compose(recv[2 * i], recv[2 * i + 1]).astype(BF16)
    for i in range(4):
        tree[8 + i] = compose(tree[2 * i], tree[2 * i + 1]).astype(BF16)
    for i in range(2):
        tree[12 + i] = compose(tree[8 + 2 * i], tree[9 + 2 * i]).astype(BF16)
    tree[14] = compose(tree[12], tree[13]).astype(BF16)

    def inside(head, carry):
        lanes = lanes_of(head)
        both = jnp.concatenate([past_rows(1, lanes, linear > 0), query_in[:, lanes].astype(F32)], 0)
        query = (rounded(weigh(both, lanes, 0)[8:]) * rise[:, lanes]).astype(BF16)
        scores = jnp.where(level[...] >= 0, dot_nt(query, key_down[:, lanes]), 0.0).astype(BF16)
        inner = dot(scores, solved_kept[head])
        inner_out[head] = inner[:, :WIDTH]
        query_state[head] = (
            (query.astype(F32) - inner[:, WIDTH:]) * vectors[0:1, lanes]
        ).astype(BF16)
        gate = 1.0 / (1.0 + jnp.exp(-gate_in[:, lanes].astype(F32)))
        gates[head] = gain_ref[...] * gate
        return carry

    def finish_inside():
        spots = [(lax.rem(x + dx, SIDE), lax.rem(y + dy, SIDE)) for dx, dy in OFFSETS[:FAR]]
        solve_own([py * SIDE + px for px, py in spots])
        lax.fori_loop(0, HEADS, inside, 0, unroll=4)

    for load in loads[5:]:
        load.wait()
    rims[1].wait_recv()

    def z_copy(source, target, sent, landed, ahead):
        return pltpu.make_async_remote_copy(
            src_ref=source,
            dst_ref=target,
            send_sem=sent,
            recv_sem=landed,
            device_id=in_line(ahead),
            device_id_type=MESH,
        )

    def pair_copy(source, ahead):
        return z_copy(source, behind, pair_send.at[ahead - 1], pair_recv, ahead)

    def state_copy(ahead):
        return z_copy(state_out, state_in, state_send.at[ahead - 1], state_recv, ahead)

    whole = tree.at[14]
    near_copy = z_copy(whole, near, near_send, near_recv, jnp.where(z == 1, 2, 1))

    @pl.when((z == 2) | (z == 4))
    def _():
        pair_copy(whole, 1).start()

    @pl.when((z == 1) | (z == 6))
    def _():
        near_copy.start()

    @pl.when(z == 0)
    def _():
        state_out[...] = tree[14, :, WIDTH:]
        state_copy(3).start()
        state_copy(1).start()
        begins[...] = jnp.zeros_like(begins)

    @pl.when((z == 3) | (z == 5))
    def _():
        pair_copy(whole, 1).wait_recv()
        tree[15] = compose(behind[...], tree[14]).astype(BF16)

    @pl.when(z == 5)
    def _():
        pair_copy(tree.at[15], 2).start()
        pair_copy(tree.at[15], 1).start()

    @pl.when(z >= 4)
    def _():
        finish_inside()

    @pl.when(z >= 6)
    def _():
        pair_copy(whole, 1).wait_recv()

    @pl.when((z == 3) | (z == 7))
    def _():
        near_copy.wait_recv()

    @pl.when(z > 0)
    def _():
        state_copy(1).wait_recv()

    @pl.when(z == 1)
    def _():
        state_out[...] = apply(tree[14], state_in[...]).astype(BF16)
        state_copy(1).start()

    @pl.when(z == 3)
    def _():
        begins[...] = apply(near[...], state_in[...]).astype(BF16)
        state_out[...] = apply(tree[15], begins[...]).astype(BF16)
        for ahead in (4, 3, 2, 1):
            state_copy(ahead).start()
        begins[...] = apply(behind[...], begins[...]).astype(BF16)

    @pl.when((z == 1) | (z == 2) | (z == 4))
    def _():
        begins[...] = state_in[...]

    @pl.when(z >= 5)
    def _():
        begins[...] = apply(behind[...], state_in[...]).astype(BF16)

    @pl.when(z == 7)
    def _():
        begins[...] = apply(near[...], begins[...]).astype(BF16)

    begin = {0: begins[...]}
    begin[8] = apply(tree[12], begin[0]).astype(BF16)
    for i in (0, 1):
        begin[8 * i + 4] = apply(tree[8 + 2 * i], begin[8 * i]).astype(BF16)
    for i in range(4):
        begin[4 * i + 2] = apply(tree[2 * i], begin[4 * i]).astype(BF16)
    for i in range(8):
        begin[2 * i + 1] = apply(recv[2 * i], begin[2 * i]).astype(BF16)
    for i in range(HEADS):
        starts[i] = begin[i]

    offsets = sorted(
        OFFSETS[: HEADS - 1], key=lambda offset: -sum(min(d, SIDE - d) for d in offset)
    )

    def down_copy(step):
        dx, dy = offsets[step]
        px, py = lax.rem(x + dx, SIDE), lax.rem(y + dy, SIDE)
        return pltpu.make_async_remote_copy(
            src_ref=starts.at[px * SIDE + py],
            dst_ref=got.at[mine],
            send_sem=down_send.at[step],
            recv_sem=down_recv.at[mine],
            device_id=in_plane(px, py),
            device_id_type=MESH,
        )

    for step in range(HEADS - 1):
        down_copy(step).start()
    got[mine] = starts[place]

    @pl.when(z < 4)
    def _():
        finish_inside()

    def await_down(head):
        pltpu.make_async_remote_copy(
            src_ref=starts.at[0],
            dst_ref=got.at[head],
            send_sem=down_send.at[0],
            recv_sem=down_recv.at[head],
            device_id=in_plane(x, y),
            device_id_type=MESH,
        ).wait_recv()

    owners = [mine]
    for dx, dy in offsets:
        owners.append(lax.rem(y + SIDE - dy, SIDE) * SIDE + lax.rem(x + SIDE - dx, SIDE))
    for part in range(SIDE):
        now = owners[SIDE * part : SIDE * part + SIDE]
        for step, head in enumerate(now):
            if part or step:
                await_down(head)
        for head in now:
            attention = inner_out[head] + dot(query_state[head], got[head])
            attention = attention.astype(BF16).astype(F32)
            scale = lax.rsqrt(jnp.mean(attention * attention, -1, keepdims=True) + 1e-05)
            out_ref[:, lanes_of(head)] = (attention * scale * gates[head]).astype(BF16)

    for copy in rims:
        copy.wait_send()

    def settle_up(slot, carry):
        up_copy(slot, x, y).wait_send()
        return carry

    lax.fori_loop(FAR, HEADS - 1, settle_up, 0)
    for copy in fars + hints:
        copy.wait_send()
    for step in range(HEADS - 1):
        down_copy(step).wait_send()

    @pl.when((z == 2) | (z == 4) | (z == 5))
    def _():
        pair_copy(whole, 1).wait_send()

    @pl.when(z == 5)
    def _():
        pair_copy(whole, 2).wait_send()

    @pl.when((z == 1) | (z == 6))
    def _():
        near_copy.wait_send()

    @pl.when((z == 0) | (z == 1) | (z == 3))
    def _():
        state_copy(1).wait_send()

    @pl.when((z == 0) | (z == 3))
    def _():
        state_copy(3).wait_send()

    @pl.when(z == 3)
    def _():
        state_copy(2).wait_send()
        state_copy(4).wait_send()


def layer(depth, query_raw, key_raw, value_raw, log_decay, beta, conv_weight, out_gate, norm_gain):
    rows, width = query_raw.shape
    wide = pltpu.VMEM((rows, width), BF16)
    more = width + FAR * WIDTH
    wider = pltpu.VMEM((rows, more), BF16)
    dma = pltpu.SemaphoreType.DMA
    return pl.pallas_call(
        functools.partial(kernel, depth),
        out_shape=jax.ShapeDtypeStruct((rows, width), BF16),
        in_specs=[pl.BlockSpec(memory_space=pltpu.HBM)] * 8,
        out_specs=pl.BlockSpec(memory_space=pltpu.VMEM),
        scratch_shapes=[wide, wider, wider, wider, wide]
        + [
            pltpu.VMEM(beta.shape[::-1], BF16),
            pltpu.VMEM(conv_weight.shape, F32),
            pltpu.VMEM((1, WIDTH), F32),
            pltpu.VMEM((FAR, HEADS, WIDTH), BF16),
            pltpu.VMEM((8, width), BF16),
            pltpu.VMEM((2, 8, more), BF16),
            pltpu.VMEM((rows, more), F32),
        ]
        + [wider] * 4
        + [
            pltpu.VMEM((2, 16, more), F32),
            pltpu.VMEM((8, more), F32),
            pltpu.VMEM((HEADS, WIDTH, WIDTH), F32),
            pltpu.VMEM((HEADS, WIDTH, WIDTH), BF16),
            pltpu.VMEM((WIDTH, WIDTH), jnp.int32),
            pltpu.VMEM((HEADS, WIDTH, 2 * WIDTH), BF16),
            pltpu.VMEM((HEADS, WIDTH, WIDTH), F32),
            pltpu.VMEM((HEADS, WIDTH, 2 * WIDTH), BF16),
            pltpu.VMEM((HEADS, WIDTH, 2 * WIDTH), BF16),
            pltpu.VMEM((16, WIDTH, 2 * WIDTH), BF16),
            pltpu.VMEM((WIDTH, 2 * WIDTH), BF16),
            pltpu.VMEM((WIDTH, 2 * WIDTH), BF16),
            pltpu.VMEM((WIDTH, WIDTH), BF16),
            pltpu.VMEM((WIDTH, WIDTH), BF16),
            pltpu.VMEM((WIDTH, WIDTH), BF16),
            pltpu.VMEM((HEADS, WIDTH, WIDTH), BF16),
            pltpu.VMEM((HEADS, WIDTH, WIDTH), BF16),
            dma((8,)),
            dma((2,)),
            dma((2,)),
            dma((FAR * FAR,)),
            dma((FAR * FAR,)),
            dma((FAR,)),
            dma((FAR,)),
            dma((HEADS,)),
            dma((HEADS,)),
            dma((2,)),
            dma,
            dma,
            dma,
            dma((4,)),
            dma,
            dma((HEADS,)),
            dma((HEADS,)),
        ],
        compiler_params=pltpu.CompilerParams(
            collective_id=0, has_side_effects=True, vmem_limit_bytes=40 * 2**20
        ),
    )(
        *[
            pltpu.with_memory_space_constraint(array, pltpu.HBM)
            for array in (
                query_raw,
                key_raw,
                value_raw,
                log_decay,
                out_gate,
                beta.T,
                conv_weight,
                norm_gain.reshape(1, WIDTH),
            )
        ]
    )


def solution(mesh):
    tokens = P(("dp", "ctx", "head"), None)
    return jax.shard_map(
        functools.partial(layer, mesh.shape["ctx"] // SIDE),
        mesh=mesh,
        in_specs=(tokens, tokens, tokens, tokens, tokens, P(), tokens, P()),
        out_specs=tokens,
        check_vma=False,
    )
```
